32 devices in a mesh: groups: 2 (over x), blk: 8 (over z, y), head: 2 (over core).
Axes of the slice: x: 2, y: 2, z: 4, core: 2. Of those that a mesh axis runs over, the one named last changes fastest.
Arguments:
- q_latent: float32 [32, 128, 512], P(('groups', 'blk'), 'head'), parts along dimension 0, may hold values from -16 to 16
- q_rope: float32 [32, 128, 64], P(('groups', 'blk'), 'head'), parts along dimension 0, may hold values from -8 to 8
- cache_latent: float32 [32768, 512], P(('groups', 'blk')), parts along dimension 0, may hold values from -8 to 8
- cache_rope: float32 [32768, 64], P(('groups', 'blk')), parts along dimension 0, may hold values from -4 to 4
- home_offset: int32 [32], P(('groups', 'blk')), parts along dimension 0, may hold values from 0 to 14335
- lengths: int32 [32], P(('groups', 'blk')), parts along dimension 0, may hold values from 1 to 14336, as said below
Outputs:
- attended: float32 [32, 128, 512], P(('groups', 'blk'), 'head'), parts along dimension 0
The draws below stay inside these ranges and needn't reach their ends.
There are 2 independent parts, one for each index of `groups`. The reference program is written for one: setup_inputs(seed, part) draws one part's arguments, and reference() takes and returns one part's arrays. A program takes and returns all parts, laid end to end along the dimension named above; each array names one. Nothing has to cross between parts.
Inputs may be any that keep to these rules, and one draw needn't show every extreme that they name: `lengths`: some query has all 14336 cells live.
All inputs are finite; a program needn't handle non-finite values.
Results may differ from the reference program's by a relative error of at most 0.0003.
Values sent between devices are 32-bit elements; how exact they have to be, the bound alone decides.
A program may use at most 64 MiB of HBM per device.

```python
import math
import jax
import jax.numpy as jnp
from jax import lax

LAT = 512
ROPE = 64
NOPE = 128
HEADS = 128
QDEV = 2
CACHE_DEV = 2048
HOPS = 3
BATCH = 16
SEQ = 16384
WINDOW = 14336


def layout(base_key):
    int_key = jax.random.fold_in(base_key, 7)
    beginnings = jax.random.randint(jax.random.fold_in(int_key, 1), (BATCH,), 0, WINDOW)
    extents = jax.random.randint(jax.random.fold_in(int_key, 2), (BATCH,), 1, WINDOW + 1)
    chosen = jax.random.randint(jax.random.fold_in(int_key, 3), (), 0, BATCH)
    query_ids = jnp.arange(BATCH)
    extents = jnp.where(query_ids == chosen, WINDOW, extents)
    return (beginnings.astype(jnp.int32), extents.astype(jnp.int32))


def tables(base_key):
    latent_key = jax.random.fold_in(base_key, 21)
    rotary_key = jax.random.fold_in(base_key, 22)
    latent = jax.random.truncated_normal(latent_key, -4.0, 4.0, (SEQ, LAT), jnp.float32)
    rotary = jax.random.truncated_normal(rotary_key, -4.0, 4.0, (SEQ, ROPE), jnp.float32)
    return (latent, rotary)


def draw_cache_latent(key, part):
    return tables(key)[0]


def draw_cache_rope(key, part):
    return tables(key)[1]


def draw_home_offset(key, part):
    return layout(key)[0]


def draw_lengths(key, part):
    return layout(key)[1]


def draw_q_latent(key, part):
    query_key = jax.random.fold_in(key, 31)
    queries = 2.0 * jax.random.truncated_normal(query_key, -4.0, 4.0, (BATCH, HEADS, LAT), jnp.float32)
    return queries


def draw_q_rope(key, part):
    query_key = jax.random.fold_in(key, 32)
    queries = 2.0 * jax.random.truncated_normal(query_key, -4.0, 4.0, (BATCH, HEADS, ROPE), jnp.float32)
    return queries


def setup_inputs(seed: int = 0, part: int = 0) -> dict:
    streams_of = jax.random.split(jax.random.key(seed), 7)
    part_keys = jax.random.split(jax.random.fold_in(streams_of[6], part), 7)
    q_latent = draw_q_latent(jax.random.fold_in(jax.random.fold_in(streams_of[6], part), 71), part)
    q_rope = draw_q_rope(jax.random.fold_in(jax.random.fold_in(streams_of[6], part), 71), part)
    cache_latent = draw_cache_latent(jax.random.fold_in(jax.random.fold_in(streams_of[6], part), 71), part)
    cache_rope = draw_cache_rope(jax.random.fold_in(jax.random.fold_in(streams_of[6], part), 71), part)
    home_offset = draw_home_offset(jax.random.fold_in(jax.random.fold_in(streams_of[6], part), 71), part)
    lengths = draw_lengths(jax.random.fold_in(jax.random.fold_in(streams_of[6], part), 71), part)
    return {"q_latent": q_latent, "q_rope": q_rope, "cache_latent": cache_latent, "cache_rope": cache_rope, "home_offset": home_offset, "lengths": lengths}


def reference(q_latent, q_rope, cache_latent, cache_rope, home_offset, lengths):
    scale = 1.0 / math.sqrt(NOPE + ROPE)
    offsets = jnp.arange(WINDOW, dtype=jnp.int32)

    def attend_one(packed):
        query, query_rope, index, beginning, extent = packed
        first_block = index // QDEV - HOPS
        positions = jnp.mod(first_block * CACHE_DEV + offsets, SEQ).astype(jnp.int32)
        keys = jnp.take(cache_latent, positions, axis=0)
        rope_keys = jnp.take(cache_rope, positions, axis=0)
        scores = (jnp.dot(query, keys.T, precision=lax.Precision.HIGHEST) + jnp.dot(query_rope, rope_keys.T, precision=lax.Precision.HIGHEST)) * scale
        validity = jnp.mod(offsets - beginning, WINDOW) < extent
        peak = lax.optimization_barrier(jnp.max(jnp.where(validity[None, :], scores, -jnp.inf), axis=1, keepdims=True))
        weights = jnp.where(validity[None, :], jnp.exp(scores - peak), 0.0)
        totals = lax.optimization_barrier(jnp.sum(weights, axis=1, keepdims=True))
        return jnp.dot(weights, keys, precision=lax.Precision.HIGHEST) / totals
    indices = jnp.arange(BATCH, dtype=jnp.int32)
    return lax.map(attend_one, (q_latent, q_rope, indices, home_offset, lengths))
```

```python
import functools
import math

import jax
import jax.numpy as jnp
from jax import lax
from jax.experimental import pallas as pl
from jax.experimental.pallas import tpu as pltpu
from jax.sharding import PartitionSpec as P

ROPE = 64
NOPE = 128
HOPS = 3

MESH = pl.DeviceIdType.MESH
FLOOR = -1e30
DEAD = -2e30
FACTOR = math.log2(math.e) / math.sqrt(NOPE + ROPE)
CHUNK = 256
LONG = 512
STEP = 256

NT = (((1,), (1,)), ((), ()))

Y, IN, OUT, OVER, CROSS, FAR = (0, 1), (1, 0), (-1, 0), (2, 0), (2, 1), (3, 0)
END, MID = 0, 1
START, REST = -1, 9
SEND, TAKE, GIVE, JOIN = range(4)
PIECES = 4
PARTS = 4
TURNS = 2
BEFORE = 5
ORDER = {
    END: ((0, 0), (1, 6), (3, 5), (2, 7)),
    MID: ((2, 2), (0, 5), (4, 1), (3, 7)),
}
PLAN = {
    (END, START, 0): (
        (SEND, 0, 0, (0,), Y),
        (SEND, 0, 0, (0,), IN),
        (SEND, 0, 0, (3,), IN),
        (SEND, 0, 0, (2,), IN),
        (SEND, 0, 0, (2,), Y),
        (SEND, 0, 0, (1,), IN),
        (SEND, 0, 0, (3,), Y),
    ),
    (END, 0, 4): (
        (SEND, 0, 0, (1,), Y),
        (TAKE, 2, 0, (0,), (Y,)),
    ),
    (END, 1, 0): (
        (TAKE, 2, 0, (1, 2, 3,), (Y,)),
        (TAKE, 6, 0, (0, 1, 2, 3,), (Y,)),
        (TAKE, 1, 0, (0, 1, 2, 3,), ()),
    ),
    (END, 1, 4): (
        (GIVE, 6, 0, (0, 1, 2, 3,), Y),
        (GIVE, 1, 0, (0, 1, 2, 3,), Y),
    ),
    (END, 2, 0): (
        (TAKE, 3, 0, (0, 1, 2, 3,), ()),
        (TAKE, 5, 0, (0, 1, 2, 3,), ()),
    ),
    (END, 2, 4): (
        (GIVE, 3, 0, (0, 1, 2, 3,), Y),
        (GIVE, 5, 0, (0, 1, 2, 3,), CROSS),
    ),
    (END, 3, 0): (
        (TAKE, 7, 0, (0, 1, 2, 3,), ()),
    ),
    (END, 3, 4): (
        (JOIN, 7, 1, (0, 1, 2, 3,), IN),
    ),
    (END, REST, 0): (
        (JOIN, 2, 1, (0,), IN),
        (JOIN, 0, 2, (0,), None),
        (JOIN, 2, 1, (1,), IN),
        (JOIN, 0, 2, (1,), None),
        (JOIN, 0, 1, (0, 1,), None),
        (JOIN, 2, 1, (2,), IN),
        (JOIN, 0, 2, (2,), None),
        (JOIN, 2, 1, (3,), IN),
        (JOIN, 0, 2, (3,), None),
        (JOIN, 0, 1, (2, 3,), None),
        (JOIN, 0, 5, (0, 1, 2, 3,), None),
    ),
    (MID, START, 0): (
        (SEND, 2, 0, (0,), IN),
        (SEND, 2, 0, (0,), Y),
        (SEND, 2, 0, (3,), OUT),
        (SEND, 2, 0, (3,), IN),
        (SEND, 2, 0, (0,), OUT),
        (SEND, 2, 0, (2,), OUT),
        (SEND, 2, 0, (1,), IN),
        (SEND, 2, 0, (2, 3,), Y),
        (SEND, 2, 0, (1,), OUT),
    ),
    (MID, 0, 1): (
        (SEND, 2, 0, (2,), IN),
    ),
    (MID, 0, 2): (
        (TAKE, 4, 0, (0,), (Y,)),
        (TAKE, 0, 0, (0,), (Y, OVER,)),
    ),
    (MID, 1, 0): (
        (TAKE, 4, 0, (1, 2, 3,), (Y,)),
        (TAKE, 0, 0, (1, 2, 3,), (Y, OVER,)),
        (TAKE, 5, 0, (0,), (OUT,)),
        (TAKE, 1, 0, (0,), (IN,)),
        (TAKE, 5, 0, (1, 2, 3,), (OUT,)),
    ),
    (MID, 1, 1): (
        (TAKE, 1, 0, (1,), (IN,)),
    ),
    (MID, 1, 2): (
        (TAKE, 1, 0, (2,), (IN,)),
    ),
    (MID, 1, 3): (
        (SEND, 2, 0, (1,), Y),
    ),
    (MID, 1, 4): (
        (GIVE, 5, 0, (0, 1, 2, 3,), Y),
        (TAKE, 1, 0, (3,), (IN,)),
    ),
    (MID, 2, 4): (
        (GIVE, 1, 0, (0, 1, 2, 3,), Y),
        (JOIN, 4, 3, (0, 1,), IN),
    ),
    (MID, 3, 0): (
        (TAKE, 3, 0, (0, 1, 2, 3,), ()),
        (TAKE, 7, 0, (0, 1, 2, 3,), ()),
    ),
    (MID, 3, 1): (
        (JOIN, 4, 3, (2, 3,), IN),
    ),
    (MID, 3, 3): (
        (JOIN, 0, 3, (0,), OUT),
        (JOIN, 2, 4, (0, 1,), None),
        (JOIN, 0, 3, (1,), OUT),
    ),
    (MID, 3, 4): (
        (GIVE, 3, 0, (0, 1, 2, 3,), Y),
        (JOIN, 0, 3, (2,), OUT),
    ),
    (MID, REST, 0): (
        (JOIN, 0, 3, (3,), OUT),
        (JOIN, 7, 0, (0, 1, 2,), CROSS),
        (JOIN, 2, 4, (2,), None),
        (JOIN, 7, 0, (3,), CROSS),
        (JOIN, 2, 4, (3,), None),
        (JOIN, 2, 3, (0,), None),
        (JOIN, 2, 7, (0,), None),
        (JOIN, 2, 0, (0,), None),
        (JOIN, 2, 3, (1,), None),
        (JOIN, 2, 7, (1,), None),
        (JOIN, 2, 0, (1,), None),
        (JOIN, 2, 3, (2,), None),
        (JOIN, 2, 7, (2,), None),
        (JOIN, 2, 0, (2,), None),
        (JOIN, 2, 3, (3,), None),
        (JOIN, 2, 7, (3,), None),
        (JOIN, 2, 0, (3,), None),
    ),
}


def landing(count, kind, link, slot):
    label, column = divmod(slot, 2)
    if kind + link[0] >= count // 2:
        label = count - 1 - label
    return 2 * label + (column + link[1]) % 2


def links_used(count):
    sent = {
        kind: {
            way
            for (k, _, _), actions in PLAN.items()
            for action, _, _, _, ways in actions
            for way in (ways if action == TAKE else (ways,))
            if k == kind and way is not None
        }
        for kind in (END, MID)
    }
    met = {kind: set(links) for kind, links in sent.items()}
    for kind, links in sent.items():
        for link in links:
            label = kind + link[0]
            label = count - 1 - label if label >= count // 2 else label
            source = landing(count, kind, link, 2 * kind) // 2
            met[label].add((source - label, link[1]))
    return {kind: sorted(links) for kind, links in met.items()}


def split(x):
    high = x.astype(jnp.bfloat16)
    low = (x - high.astype(jnp.float32)).astype(jnp.bfloat16)
    return high, low


def prepare_cache(cache_ref, rope_ref, kcat, vt_hi, vt_lo, fetch=None, first=0, last=None):
    cells, width = cache_ref.shape
    step = STEP

    def body(i, _):
        if fetch is not None:
            fetch(i).wait()
        rows = pl.ds(pl.multiple_of(i * step, step), step)
        block = cache_ref[rows, :]
        high, low = split(block)
        kcat[rows, 0:width] = high
        kcat[rows, width : 2 * width] = low
        turned = block.T
        t_high, t_low = split(turned)
        vt_hi[:, rows] = t_high
        vt_lo[:, rows] = t_low
        rope = rope_ref[:, rows].T
        r_high = rope.astype(jnp.bfloat16).astype(jnp.float32)
        r_low = rope - r_high
        wide = jnp.concatenate([r_high, r_high, r_low, jnp.zeros_like(rope)], axis=1)
        kcat[rows, 2 * width : 2 * width + 4 * rope.shape[1]] = wide.astype(jnp.bfloat16)
        return 0

    lax.fori_loop(first, cells // step if last is None else last, body, 0)


def rope_rows(aux, heads):
    packed = aux[0:heads, :] * FACTOR
    high = packed.astype(jnp.bfloat16).astype(jnp.float32)
    low = packed - high
    half = packed.shape[1] // 2
    blank = jnp.zeros((heads, half), jnp.float32)
    rows = []
    for part in (slice(0, half), slice(half, 2 * half)):
        rows.append(jnp.concatenate([high[:, part], low[:, part], high[:, part], blank], axis=1))
    return jnp.concatenate(rows, axis=0).astype(jnp.bfloat16)


def visit(parts, kcat, vt_hi, vt_lo, s_ref, ph_ref, pl_ref, window):
    cells = kcat.shape[0]
    width = vt_hi.shape[0]
    heads = parts[0][1].shape[0] - 8
    query = jnp.concatenate([p[0] for p in parts], axis=0) * FACTOR
    q_hi, q_lo = split(query)
    rope = jnp.concatenate([rope_rows(p[1], heads) for p in parts], axis=0)
    q_cat = jnp.concatenate([q_hi, q_hi, rope], axis=1)
    starts = jnp.concatenate([p[1][heads : heads + 1, :] - p[2] for p in parts], axis=1)
    extents = jnp.concatenate([p[1][heads + 1 : heads + 2, :] * p[3] for p in parts], axis=1)
    ends = starts + extents
    wrapped = ends - window
    count = query.shape[0]
    peak = jnp.full((1, count), FLOOR, jnp.float32)
    for c in range(cells // CHUNK):
        rows = slice(c * CHUNK, (c + 1) * CHUNK)
        scores = lax.dot_general(kcat[rows, :], q_cat, NT, preferred_element_type=jnp.float32)
        scores += lax.dot_general(
            kcat[rows, 0:width], q_lo, NT, preferred_element_type=jnp.float32
        )
        cell = lax.broadcasted_iota(jnp.int32, (CHUNK, count), 0).astype(jnp.float32) + c * CHUNK
        live = ((cell >= starts) & (cell < ends)) | (cell < wrapped)
        scores = jnp.where(live, scores, DEAD)
        s_ref[rows, 0:count] = scores
        peak = jnp.maximum(peak, jnp.max(scores, axis=0, keepdims=True))
    total = jnp.zeros((1, count), jnp.float32)
    summed = None
    for c in range(cells // CHUNK):
        rows = slice(c * CHUNK, (c + 1) * CHUNK)
        weights = jnp.exp2(s_ref[rows, 0:count] - peak)
        total += jnp.sum(weights, axis=0, keepdims=True)
        high, low = split(weights)
        ph_ref[rows, 0:count] = high
        pl_ref[rows, 0:count] = low
    high = ph_ref[:, 0:count]
    summed = jnp.dot(vt_hi[...], high, preferred_element_type=jnp.float32)
    summed += jnp.dot(vt_hi[...], pl_ref[:, 0:count], preferred_element_type=jnp.float32)
    summed += jnp.dot(vt_lo[...], high, preferred_element_type=jnp.float32)
    return summed, peak, total


def window_kernel(
    size,
    q_ref, aux_ref, cache_ref, rope_ref, out_ref,
    kcat, vt_hi, vt_lo, s_ref, ph_ref, pl_ref,
    q_got, aux_got, sums, stats, sums_got, stats_got,
    q_send, q_recv, a_send, a_recv, o_send, o_recv, t_send, t_recv,
):
    me = lax.axis_index("blk")
    cells = cache_ref.shape[0]
    window = (2 * HOPS + 1) * cells
    distances = [sign * k for k in range(1, HOPS + 1) for sign in (1, -1)]

    def device(distance):
        return {"blk": lax.rem(me + distance + size, size)}

    barrier = pltpu.get_barrier_semaphore()
    for d in distances:
        pl.semaphore_signal(barrier, inc=1, device_id=device(d), device_id_type=MESH)
    pl.semaphore_wait(barrier, 2 * HOPS)

    sent = []
    for i, d in enumerate(distances):
        for source, target, send, recv in (
            (q_ref, q_got, q_send, q_recv),
            (aux_ref, aux_got, a_send, a_recv),
        ):
            copy = pltpu.make_async_remote_copy(
                src_ref=source, dst_ref=target.at[i], send_sem=send.at[i], recv_sem=recv.at[i],
                device_id=device(d), device_id_type=MESH,
            )
            copy.start()
            sent.append(copy)

    prepare_cache(cache_ref, rope_ref, kcat, vt_hi, vt_lo)
    run = functools.partial(
        visit, kcat=kcat, vt_hi=vt_hi, vt_lo=vt_lo, s_ref=s_ref, ph_ref=ph_ref, pl_ref=pl_ref,
        window=window,
    )
    rows = q_ref.shape[0]
    own = run([(q_ref[...], aux_ref[...], float(HOPS * cells), 1.0)])
    sums[2 * HOPS, :, :] = own[0]
    stats[2 * HOPS, 0:1, :] = own[1]
    stats[2 * HOPS, 1:2, :] = own[2]

    def pair(k, _):
        parts = []
        for j, sign in ((0, 1), (1, -1)):
            i = 2 * k + j
            for source, target, send, recv in (
                (q_ref, q_got, q_send, q_recv),
                (aux_ref, aux_got, a_send, a_recv),
            ):
                pltpu.make_async_remote_copy(
                    src_ref=source, dst_ref=target.at[i], send_sem=send.at[i], recv_sem=recv.at[i],
                    device_id=device(1), device_id_type=MESH,
                ).wait_recv()
            slot = HOPS + sign * (k + 1)
            parts.append((q_got[i], aux_got[i], (slot * cells).astype(jnp.float32), 1.0))
        summed, peak, total = run(parts)
        for j, sign in ((0, 1), (1, -1)):
            i = 2 * k + j
            lanes = slice(j * rows, (j + 1) * rows)
            sums[i, :, :] = summed[:, lanes]
            stats[i, 0:1, :] = peak[:, lanes]
            stats[i, 1:2, :] = total[:, lanes]
            for source, target, send, recv in (
                (sums, sums_got, o_send, o_recv),
                (stats, stats_got, t_send, t_recv),
            ):
                pltpu.make_async_remote_copy(
                    src_ref=source.at[i], dst_ref=target.at[i],
                    send_sem=send.at[i], recv_sem=recv.at[i],
                    device_id=device(-sign * (k + 1)), device_id_type=MESH,
                ).start()
        return 0

    lax.fori_loop(0, HOPS, pair, 0)

    for i in range(2 * HOPS):
        for source, target, send, recv in (
            (sums, sums_got, o_send, o_recv),
            (stats, stats_got, t_send, t_recv),
        ):
            copy = pltpu.make_async_remote_copy(
                src_ref=source.at[i], dst_ref=target.at[i],
                send_sem=send.at[i], recv_sem=recv.at[i],
                device_id=device(1), device_id_type=MESH,
            )
            copy.wait_recv()
            copy.wait_send()

    for copy in sent:
        copy.wait_send()

    peak = stats[2 * HOPS, 0:1, :]
    for i in range(2 * HOPS):
        peak = jnp.maximum(peak, stats_got[i, 0:1, :])
    factors = [jnp.exp2(stats[2 * HOPS, 0:1, :] - peak)]
    total = stats[2 * HOPS, 1:2, :] * factors[0]
    for i in range(2 * HOPS):
        factors.append(jnp.exp2(stats_got[i, 0:1, :] - peak))
        total += stats_got[i, 1:2, :] * factors[i + 1]
    width = sums.shape[1]
    for c in range(0, width, 128):
        piece = sums[2 * HOPS, c : c + 128, :] * factors[0]
        for i in range(2 * HOPS):
            piece += sums_got[i, c : c + 128, :] * factors[i + 1]
        out_ref[:, c : c + 128] = (piece / total).T


def line_kernel(
    size,
    q_ref, q_rope_ref, home_ref, length_ref, cache_hbm, rope_ref, out_ref,
    kcat, vt_hi, vt_lo, s_ref, ph_ref, pl_ref,
    cache, q_all, aux_all, acc, got, fac,
    fetch_sem, own_sem, q_send, q_recv, r_send, r_recv,
):
    me = lax.axis_index("blk")
    count = size // 2
    z, y = me // 2, lax.rem(me, 2)
    far = z >= count // 2
    end = (z == 0) | (z == count - 1)
    inward = jnp.where(far, -1, 1)
    cells, width = cache.shape
    rows = q_ref.shape[0]
    window = (2 * HOPS + 1) * cells
    tall = rows // PIECES
    met = links_used(count)
    ways = sorted({link for links in met.values() for link in links})
    devices = {
        link: {
            "blk": 2 * jnp.clip(z + link[0] * inward, 0, count - 1) + (1 - y if link[1] else y)
        }
        for link in ways
    }

    def remote(source, target, send, recv, link):
        return pltpu.make_async_remote_copy(
            src_ref=source, dst_ref=target, send_sem=send, recv_sem=recv,
            device_id=devices[link], device_id_type=MESH,
        )

    def q_part(slot, p):
        if p == PIECES:
            return aux_all.at[slot]
        return q_all.at[slot, pl.ds(p * tall, tall)]

    def q_copy(kind, link, slot, p):
        there = landing(count, kind, link, slot)
        return remote(
            q_part(slot, p), q_part(there, p), q_send.at[ways.index(link), slot, p], q_recv.at[there, p], link
        )

    def parts_of(p):
        return (PIECES, 0) if p == 0 else (p,)

    def q_start(kind, link, slot, p):
        for part in parts_of(p):
            q_copy(kind, link, slot, part).start()

    def q_wait(slot, p):
        for part in parts_of(p):
            piece = q_part(slot, part)
            remote(piece, piece, q_send.at[0, slot, part], q_recv.at[slot, part], Y).wait_recv()

    def r_part(ref, k):
        return ref.at[pl.ds(0, 8 + deep)] if k == 0 else ref.at[pl.ds(8 + k * deep, deep)]

    deep = width // PARTS

    sides = list(range(size))

    def r_copy(kind, link, slot, k):
        there = landing(count, kind, link, slot)
        side = sides.index(landing(count, kind, link, 2 * kind))
        return remote(
            r_part(acc.at[slot], k), r_part(got.at[side, there], k),
            r_send.at[slot, k], r_recv.at[side, there, k], link,
        )

    def merge(slot, side, k):
        piece = r_part(got.at[side, slot], k)
        remote(piece, piece, r_send.at[slot, k], r_recv.at[side, slot, k], Y).wait_recv()
        if k == 0:
            first, second = acc[slot, 0:1, :], got[side, slot, 0:1, :]
            peak = jnp.maximum(first, second)
            first, second = jnp.exp2(first - peak), jnp.exp2(second - peak)
            total = acc[slot, 1:2, :] * first + got[side, slot, 1:2, :] * second
            acc[slot, 0:1, :] = peak
            acc[slot, 1:2, :] = total
            fac[side, slot, 0:1, :] = first
            fac[side, slot, 1:2, :] = second
        else:
            first, second = fac[side, slot, 0:1, :], fac[side, slot, 1:2, :]
        lines = slice(8 + k * deep, 8 + (k + 1) * deep)
        acc[slot, lines, :] = acc[slot, lines, :] * first + got[side, slot, lines, :] * second

    sent_q, sent_r = {END: [], MID: []}, {END: [], MID: []}

    def perform(kind, actions, note):
        for action, slot, source, pieces, link in actions:
            for p in pieces:
                if action == TAKE:
                    q_wait(slot, p)
                if action == JOIN:
                    merge(slot, source, p)
                for way in link if action == TAKE else () if link is None else (link,):
                    if action in (SEND, TAKE):
                        q_start(kind, way, slot, p)
                        note[0].extend((way, slot, part) for part in parts_of(p))
                    else:
                        r_copy(kind, way, slot, p).start()
                        note[1].append((way, slot, p))

    kinds = ((END, end), (MID, jnp.logical_not(end)))

    def run(point, stages, visit=None):
        for kind, here in kinds:
            due = [(k, PLAN[kind, k, point]) for k in stages if (kind, k, point) in PLAN]
            if due:

                @pl.when(here)
                def _(kind=kind, due=due):
                    for k, actions in due:
                        note = (sent_q[kind], sent_r[kind])
                        if visit is None:
                            perform(kind, actions, note)
                        else:
                            pl.when(visit == k)(
                                functools.partial(perform, kind, actions, note)
                            )

    mine = jnp.where(end, 0, 2)
    own_copy = pltpu.make_async_copy(q_ref, q_all.at[mine], own_sem.at[0])
    own_copy.start()

    def fetch(i):
        part = pl.ds(pl.multiple_of(i * STEP, STEP), STEP)
        return pltpu.make_async_copy(cache_hbm.at[part], cache.at[part], fetch_sem.at[i])

    for i in range(cells // STEP):
        fetch(i).start()

    barrier = pltpu.get_barrier_semaphore()
    for kind, here in kinds:

        @pl.when(here)
        def _(kind=kind):
            for link in met[kind]:
                pl.semaphore_signal(
                    barrier, inc=1, device_id=devices[link], device_id_type=MESH
                )

    height, heads, _ = q_rope_ref.shape
    packed = jnp.concatenate([q_rope_ref[i] for i in range(height)], axis=1)
    aux_all[mine, 0:heads, :] = packed
    line = lax.broadcasted_iota(jnp.int32, (8, rows), 0)
    lane = lax.broadcasted_iota(jnp.int32, (8, rows), 1)
    meta = jnp.zeros((8, rows), jnp.float32)
    for i in range(height):
        values = jnp.where(
            line == 0, home_ref[i].astype(jnp.float32), length_ref[i].astype(jnp.float32)
        )
        meta = jnp.where((lane >= i * heads) & (line < 2), values, meta)
    aux_all[mine, heads : heads + 8, :] = meta

    prepare = functools.partial(prepare_cache, cache, rope_ref, kcat, vt_hi, vt_lo, fetch)
    prepare(0, BEFORE)
    own_copy.wait()
    pl.semaphore_wait(barrier, jnp.where(end, len(met[END]), len(met[MID])))
    run(0, (START,))
    prepare(BEFORE, cells // STEP)

    def pick(i, c):
        chosen = jnp.int32(0)
        for kind, here in kinds:
            for k, pair in enumerate(ORDER[kind]):
                chosen = jnp.where(here & (i == k), pair[c], chosen)
        return chosen

    def step(i, _):
        def hook(point):
            run(point, range(len(ORDER[END])), i)

        hook(0)
        parts, slots = [], []
        for c in range(2):
            slot = pick(i, c)
            label = slot // 2
            block = 2 * jnp.where(far, count - 1 - label, label)
            block += jnp.where(lax.rem(slot, 2) == 0, y, 1 - y)
            place = lax.rem(me - block + HOPS + size, size)
            parts.append((q_all[slot], aux_all[slot], (place * cells).astype(jnp.float32)))
            slots.append(slot)
        visit_line(parts, kcat, vt_hi, vt_lo, s_ref, ph_ref, pl_ref, window, acc, slots, hook)
        return 0

    lax.fori_loop(0, len(ORDER[END]), step, 0)
    run(0, (REST,))

    def result(own):
        total = acc[own, 1:2, :]
        for c in range(0, width, 128):
            out_ref[:, c : c + 128] = (acc[own, 8 + c : 8 + c + 128, :] / total).T

    for kind, here in kinds:

        @pl.when(here)
        def _(kind=kind):
            result(0 if kind == END else 2)
            for link, slot, part in sent_q[kind]:
                q_copy(kind, link, slot, part).wait_send()
            for link, slot, k in sent_r[kind]:
                r_copy(kind, link, slot, k).wait_send()


def visit_line(parts, kcat, vt_hi, vt_lo, s_ref, ph_ref, pl_ref, window, acc, slots, hook):
    cells = kcat.shape[0]
    width = vt_hi.shape[0]
    heads = parts[0][1].shape[0] - 8
    query = jnp.concatenate([p[0] for p in parts], axis=0) * FACTOR
    q_hi, q_lo = split(query)
    rope = jnp.concatenate([rope_rows(p[1], heads) for p in parts], axis=0)
    q_cat = jnp.concatenate([q_hi, q_hi, rope], axis=1)
    starts = jnp.concatenate([p[1][heads : heads + 1, :] - p[2] for p in parts], axis=1)
    extents = jnp.concatenate([p[1][heads + 1 : heads + 2, :] for p in parts], axis=1)
    ends = starts + extents
    wrapped = ends - window
    count = query.shape[0]
    rows = count // 2
    peak = jnp.full((1, count), FLOOR, jnp.float32)
    chunks = cells // LONG
    for c in range(chunks):
        lines = slice(c * LONG, (c + 1) * LONG)
        scores = lax.dot_general(kcat[lines, :], q_cat, NT, preferred_element_type=jnp.float32)
        scores += lax.dot_general(
            kcat[lines, 0:width], q_lo, NT, preferred_element_type=jnp.float32
        )
        cell = lax.broadcasted_iota(jnp.int32, (LONG, count), 0).astype(jnp.float32) + c * LONG
        live = ((cell >= starts) & (cell < ends)) | (cell < wrapped)
        scores = jnp.where(live, scores, DEAD)
        s_ref[lines, :] = scores
        peak = jnp.maximum(peak, jnp.max(scores, axis=0, keepdims=True))
    hook(1)
    total = jnp.zeros((1, count), jnp.float32)
    for c in range(chunks):
        lines = slice(c * LONG, (c + 1) * LONG)
        weights = jnp.exp2(s_ref[lines, :] - peak)
        total += jnp.sum(weights, axis=0, keepdims=True)
        high, low = split(weights)
        ph_ref[lines, :] = high
        pl_ref[lines, :] = low
    for j, slot in enumerate(slots):
        lanes = slice(j * rows, (j + 1) * rows)
        acc[slot, 0:1, :] = peak[:, lanes]
        acc[slot, 1:2, :] = total[:, lanes]
    hook(2)
    turn = width // TURNS
    for h in range(TURNS):
        feats = slice(h * turn, (h + 1) * turn)
        summed = jnp.dot(vt_hi[feats, :], ph_ref[...], preferred_element_type=jnp.float32)
        summed += jnp.dot(vt_hi[feats, :], pl_ref[...], preferred_element_type=jnp.float32)
        summed += jnp.dot(vt_lo[feats, :], ph_ref[...], preferred_element_type=jnp.float32)
        for j, slot in enumerate(slots):
            lanes = slice(j * rows, (j + 1) * rows)
            acc[slot, 8 + h * turn : 8 + (h + 1) * turn, :] = summed[:, lanes]
        hook(3 + h)


def pack_aux(q_rope, home_offset, lengths):
    height, heads, rope = q_rope.shape
    packed = jnp.concatenate([q_rope[i] for i in range(height)], axis=1)
    meta = jnp.stack([home_offset, lengths]).astype(jnp.float32)
    meta = jnp.repeat(meta, heads, axis=1)
    return jnp.concatenate([packed, meta, jnp.zeros((6, height * heads), jnp.float32)], axis=0)


def shards(size, q_latent, q_rope, cache_latent, cache_rope, home_offset, lengths):
    height, heads, width = q_latent.shape
    cells, rope = cache_rope.shape
    rows = height * heads
    flat = q_latent.reshape(rows, width)
    rope_turned = cache_rope.T
    dma = pltpu.SemaphoreType.DMA
    vmem, anywhere = (pl.BlockSpec(memory_space=m) for m in (pltpu.VMEM, pl.ANY))
    working = [
        pltpu.VMEM((cells, 2 * width + 4 * rope), jnp.bfloat16),
        pltpu.VMEM((width, cells), jnp.bfloat16),
        pltpu.VMEM((width, cells), jnp.bfloat16),
        pltpu.VMEM((cells, 2 * rows), jnp.float32),
        pltpu.VMEM((cells, 2 * rows), jnp.bfloat16),
        pltpu.VMEM((cells, 2 * rows), jnp.bfloat16),
    ]
    if size == 2 * HOPS + 2:
        kernel = line_kernel
        smem = pl.BlockSpec(memory_space=pltpu.SMEM)
        in_specs = [anywhere, vmem, smem, smem, anywhere, vmem]
        operands = (flat, q_rope, home_offset, lengths, cache_latent, rope_turned)
        ways = {link for links in links_used(size // 2).values() for link in links}
        scratch = [
            pltpu.VMEM((cells, width), jnp.float32),
            pltpu.VMEM((size, rows, width), jnp.float32),
            pltpu.VMEM((size, heads + 8, rows), jnp.float32),
            pltpu.VMEM((size, width + 8, rows), jnp.float32),
            pltpu.VMEM((size, size, width + 8, rows), jnp.float32),
            pltpu.VMEM((size, size, 8, rows), jnp.float32),
            dma((cells // STEP,)),
            dma((1,)),
            dma((len(ways), size, PIECES + 1)),
            dma((size, PIECES + 1)),
            dma((size, PARTS)),
            dma((size, size, PARTS)),
        ]
    else:
        kernel = window_kernel
        n = 2 * HOPS
        in_specs = [vmem] * 4
        operands = (flat, pack_aux(q_rope, home_offset, lengths), cache_latent, rope_turned)
        scratch = [
            pltpu.VMEM((n, rows, width), jnp.float32),
            pltpu.VMEM((n, heads + 8, rows), jnp.float32),
            pltpu.VMEM((n + 1, width, rows), jnp.float32),
            pltpu.VMEM((n + 1, 8, rows), jnp.float32),
            pltpu.VMEM((n, width, rows), jnp.float32),
            pltpu.VMEM((n, 8, rows), jnp.float32),
        ] + [dma((n,))] * 8
    out = pl.pallas_call(
        functools.partial(kernel, size),
        out_shape=jax.ShapeDtypeStruct((rows, width), jnp.float32),
        in_specs=in_specs,
        out_specs=vmem,
        scratch_shapes=working + scratch,
        compiler_params=pltpu.CompilerParams(
            collective_id=0, has_side_effects=True, vmem_limit_bytes=60 * 1024 * 1024
        ),
    )(*operands)
    return out.reshape(height, heads, width)


def solution(mesh):
    return jax.shard_map(
        functools.partial(shards, mesh.shape["blk"]),
        mesh=mesh,
        in_specs=(
            P(("groups", "blk"), "head", None),
            P(("groups", "blk"), "head", None),
            P(("groups", "blk"), None),
            P(("groups", "blk"), None),
            P(("groups", "blk")),
            P(("groups", "blk")),
        ),
        out_specs=P(("groups", "blk"), "head", None),
        check_vma=False,
    )
```

```python
import functools
import math

import jax
import jax.numpy as jnp
from jax import lax
from jax.experimental import pallas as pl
from jax.experimental.pallas import tpu as pltpu
from jax.sharding import PartitionSpec as P

ROPE = 64
NOPE = 128
HOPS = 3

MESH = pl.DeviceIdType.MESH
FLOOR = -1e30
DEAD = -2e30
FACTOR = math.log2(math.e) / math.sqrt(NOPE + ROPE)
CHUNK = 256
LONG = 512
STEP = 256

NT = (((1,), (1,)), ((), ()))

Y, IN, OUT, OVER, CROSS, FAR = (0, 1), (1, 0), (-1, 0), (2, 0), (2, 1), (3, 0)
END, MID = 0, 1
START, REST = -1, 9
SEND, TAKE, GIVE, JOIN = range(4)
PIECES = 4
PARTS = 4
TURNS = 2
BEFORE = 5
ORDER = {
    END: ((0, 0), (1, 6), (5, 3), (7, 2)),
    MID: ((2, 2), (5, 4), (0, 1), (3, 7)),
}
PLAN = {
    (END, START, 0): (
        (SEND, 0, 0, (3,), Y),
        (SEND, 0, 0, (1,), Y),
        (SEND, 0, 0, (3,), IN),
        (SEND, 0, 0, (1,), IN),
        (SEND, 0, 0, (0,), Y),
        (SEND, 0, 0, (2,), IN),
        (SEND, 0, 0, (2,), Y),
        (SEND, 0, 0, (0,), IN),
    ),
    (END, 0, 2): (
        (TAKE, 2, 0, (0,), (Y,)),
    ),
    (END, 0, 4): (
        (TAKE, 2, 0, (1,), (Y,)),
    ),
    (END, 1, 0): (
        (TAKE, 2, 0, (2, 3,), (Y,)),
        (TAKE, 6, 0, (0, 1, 2, 3,), (Y,)),
        (TAKE, 1, 0, (0, 1, 2, 3,), ()),
    ),
    (END, 1, 4): (
        (GIVE, 1, 0, (0, 1, 2, 3,), Y),
        (GIVE, 6, 0, (0, 1, 2, 3,), Y),
    ),
    (END, 2, 0): (
        (TAKE, 3, 0, (0, 1, 2, 3,), ()),
        (TAKE, 5, 0, (0, 1, 2, 3,), ()),
    ),
    (END, 2, 4): (
        (GIVE, 3, 0, (0, 1, 2, 3,), Y),
        (GIVE, 5, 0, (0, 1, 2, 3,), CROSS),
    ),
    (END, 3, 0): (
        (TAKE, 7, 0, (0, 1, 2, 3,), ()),
    ),
    (END, 3, 4): (
        (JOIN, 7, 1, (0, 1, 2,), IN),
    ),
    (END, REST, 0): (
        (JOIN, 7, 1, (3,), IN),
        (JOIN, 0, 2, (0,), None),
        (JOIN, 2, 1, (0,), IN),
        (JOIN, 0, 2, (1,), None),
        (JOIN, 0, 1, (0, 1,), None),
        (JOIN, 2, 1, (1,), IN),
        (JOIN, 0, 2, (2,), None),
        (JOIN, 2, 1, (2,), IN),
        (JOIN, 0, 2, (3,), None),
        (JOIN, 0, 1, (2, 3,), None),
        (JOIN, 2, 1, (3,), IN),
        (JOIN, 0, 5, (0, 1, 2, 3,), None),
    ),
    (MID, START, 0): (
        (SEND, 2, 0, (2,), Y),
        (SEND, 2, 0, (0, 1,), IN),
        (SEND, 2, 0, (0,), OUT),
        (SEND, 2, 0, (2,), IN),
        (SEND, 2, 0, (0,), Y),
        (SEND, 2, 0, (1,), OUT),
        (SEND, 2, 0, (3,), OUT),
        (SEND, 2, 0, (3,), IN),
        (SEND, 2, 0, (2,), OUT),
        (SEND, 2, 0, (1,), Y),
    ),
    (MID, 0, 2): (
        (TAKE, 4, 0, (0, 1,), (Y,)),
    ),
    (MID, 0, 4): (
        (TAKE, 4, 0, (2,), (Y,)),
    ),
    (MID, 1, 0): (
        (TAKE, 4, 0, (3,), (Y,)),
        (TAKE, 0, 0, (0, 1, 2, 3,), (Y, OVER,)),
        (TAKE, 5, 0, (0, 1, 2, 3,), (OUT,)),
    ),
    (MID, 1, 2): (
        (TAKE, 1, 0, (0, 1,), (IN,)),
    ),
    (MID, 1, 4): (
        (GIVE, 5, 0, (0, 1, 2, 3,), Y),
        (TAKE, 1, 0, (2, 3,), (IN,)),
    ),
    (MID, 2, 2): (
        (SEND, 2, 0, (3,), Y),
        (JOIN, 4, 3, (0,), IN),
    ),
    (MID, 2, 4): (
        (GIVE, 1, 0, (0, 1, 2, 3,), Y),
        (JOIN, 4, 3, (1, 2,), IN),
    ),
    (MID, 3, 0): (
        (JOIN, 4, 3, (3,), IN),
        (TAKE, 3, 0, (0, 1, 2, 3,), ()),
        (TAKE, 7, 0, (0, 1, 2, 3,), ()),
    ),
    (MID, 3, 2): (
        (JOIN, 0, 3, (0, 1, 2,), OUT),
    ),
    (MID, 3, 4): (
        (GIVE, 3, 0, (0, 1, 2, 3,), Y),
        (JOIN, 0, 3, (3,), OUT),
    ),
    (MID, REST, 0): (
        (JOIN, 2, 7, (0, 1,), None),
        (JOIN, 7, 0, (0,), CROSS),
        (JOIN, 2, 7, (2,), None),
        (JOIN, 7, 0, (1,), CROSS),
        (JOIN, 2, 7, (3,), None),
        (JOIN, 7, 0, (2,), CROSS),
        (JOIN, 2, 3, (0,), None),
        (JOIN, 2, 4, (0,), None),
        (JOIN, 7, 0, (3,), CROSS),
        (JOIN, 2, 3, (1,), None),
        (JOIN, 2, 4, (1,), None),
        (JOIN, 2, 0, (0,), None),
        (JOIN, 2, 3, (2,), None),
        (JOIN, 2, 4, (2,), None),
        (JOIN, 2, 0, (1,), None),
        (JOIN, 2, 3, (3,), None),
        (JOIN, 2, 4, (3,), None),
        (JOIN, 2, 0, (2, 3,), None),
    ),
}


def landing(count, kind, link, slot):
    label, column = divmod(slot, 2)
    if kind + link[0] >= count // 2:
        label = count - 1 - label
    return 2 * label + (column + link[1]) % 2


def links_used(count):
    sent = {
        kind: {
            way
            for (k, _, _), actions in PLAN.items()
            for action, _, _, _, ways in actions
            for way in (ways if action == TAKE else (ways,))
            if k == kind and way is not None
        }
        for kind in (END, MID)
    }
    met = {kind: set(links) for kind, links in sent.items()}
    for kind, links in sent.items():
        for link in links:
            label = kind + link[0]
            label = count - 1 - label if label >= count // 2 else label
            source = landing(count, kind, link, 2 * kind) // 2
            met[label].add((source - label, link[1]))
    return {kind: sorted(links) for kind, links in met.items()}


def split(x):
    high = x.astype(jnp.bfloat16)
    low = (x - high.astype(jnp.float32)).astype(jnp.bfloat16)
    return high, low


def prepare_cache(cache_ref, rope_ref, kcat, vt_hi, vt_lo, fetch=None, first=0, last=None):
    cells, width = cache_ref.shape
    step = STEP

    def body(i, _):
        if fetch is not None:
            fetch(i).wait()
        rows = pl.ds(pl.multiple_of(i * step, step), step)
        block = cache_ref[rows, :]
        high, low = split(block)
        kcat[rows, 0:width] = high
        kcat[rows, width : 2 * width] = low
        turned = block.T
        t_high, t_low = split(turned)
        vt_hi[:, rows] = t_high
        vt_lo[:, rows] = t_low
        rope = rope_ref[:, rows].T
        r_high = rope.astype(jnp.bfloat16).astype(jnp.float32)
        r_low = rope - r_high
        wide = jnp.concatenate([r_high, r_high, r_low, jnp.zeros_like(rope)], axis=1)
        kcat[rows, 2 * width : 2 * width + 4 * rope.shape[1]] = wide.astype(jnp.bfloat16)
        return 0

    lax.fori_loop(first, cells // step if last is None else last, body, 0)


def rope_rows(aux, heads):
    packed = aux[0:heads, :] * FACTOR
    high = packed.astype(jnp.bfloat16).astype(jnp.float32)
    low = packed - high
    half = packed.shape[1] // 2
    blank = jnp.zeros((heads, half), jnp.float32)
    rows = []
    for part in (slice(0, half), slice(half, 2 * half)):
        rows.append(jnp.concatenate([high[:, part], low[:, part], high[:, part], blank], axis=1))
    return jnp.concatenate(rows, axis=0).astype(jnp.bfloat16)


def visit(parts, kcat, vt_hi, vt_lo, s_ref, ph_ref, pl_ref, window):
    cells = kcat.shape[0]
    width = vt_hi.shape[0]
    heads = parts[0][1].shape[0] - 8
    query = jnp.concatenate([p[0] for p in parts], axis=0) * FACTOR
    q_hi, q_lo = split(query)
    rope = jnp.concatenate([rope_rows(p[1], heads) for p in parts], axis=0)
    q_cat = jnp.concatenate([q_hi, q_hi, rope], axis=1)
    starts = jnp.concatenate([p[1][heads : heads + 1, :] - p[2] for p in parts], axis=1)
    extents = jnp.concatenate([p[1][heads + 1 : heads + 2, :] * p[3] for p in parts], axis=1)
    ends = starts + extents
    wrapped = ends - window
    count = query.shape[0]
    peak = jnp.full((1, count), FLOOR, jnp.float32)
    for c in range(cells // CHUNK):
        rows = slice(c * CHUNK, (c + 1) * CHUNK)
        scores = lax.dot_general(kcat[rows, :], q_cat, NT, preferred_element_type=jnp.float32)
        scores += lax.dot_general(
            kcat[rows, 0:width], q_lo, NT, preferred_element_type=jnp.float32
        )
        cell = lax.broadcasted_iota(jnp.int32, (CHUNK, count), 0).astype(jnp.float32) + c * CHUNK
        live = ((cell >= starts) & (cell < ends)) | (cell < wrapped)
        scores = jnp.where(live, scores, DEAD)
        s_ref[rows, 0:count] = scores
        peak = jnp.maximum(peak, jnp.max(scores, axis=0, keepdims=True))
    total = jnp.zeros((1, count), jnp.float32)
    summed = None
    for c in range(cells // CHUNK):
        rows = slice(c * CHUNK, (c + 1) * CHUNK)
        weights = jnp.exp2(s_ref[rows, 0:count] - peak)
        total += jnp.sum(weights, axis=0, keepdims=True)
        high, low = split(weights)
        ph_ref[rows, 0:count] = high
        pl_ref[rows, 0:count] = low
    high = ph_ref[:, 0:count]
    summed = jnp.dot(vt_hi[...], high, preferred_element_type=jnp.float32)
    summed += jnp.dot(vt_hi[...], pl_ref[:, 0:count], preferred_element_type=jnp.float32)
    summed += jnp.dot(vt_lo[...], high, preferred_element_type=jnp.float32)
    return summed, peak, total


def window_kernel(
    size,
    q_ref, aux_ref, cache_ref, rope_ref, out_ref,
    kcat, vt_hi, vt_lo, s_ref, ph_ref, pl_ref,
    q_got, aux_got, sums, stats, sums_got, stats_got,
    q_send, q_recv, a_send, a_recv, o_send, o_recv, t_send, t_recv,
):
    me = lax.axis_index("blk")
    cells = cache_ref.shape[0]
    window = (2 * HOPS + 1) * cells
    distances = [sign * k for k in range(1, HOPS + 1) for sign in (1, -1)]

    def device(distance):
        return {"blk": lax.rem(me + distance + size, size)}

    barrier = pltpu.get_barrier_semaphore()
    for d in distances:
        pl.semaphore_signal(barrier, inc=1, device_id=device(d), device_id_type=MESH)
    pl.semaphore_wait(barrier, 2 * HOPS)

    sent = []
    for i, d in enumerate(distances):
        for source, target, send, recv in (
            (q_ref, q_got, q_send, q_recv),
            (aux_ref, aux_got, a_send, a_recv),
        ):
            copy = pltpu.make_async_remote_copy(
                src_ref=source, dst_ref=target.at[i], send_sem=send.at[i], recv_sem=recv.at[i],
                device_id=device(d), device_id_type=MESH,
            )
            copy.start()
            sent.append(copy)

    prepare_cache(cache_ref, rope_ref, kcat, vt_hi, vt_lo)
    run = functools.partial(
        visit, kcat=kcat, vt_hi=vt_hi, vt_lo=vt_lo, s_ref=s_ref, ph_ref=ph_ref, pl_ref=pl_ref,
        window=window,
    )
    rows = q_ref.shape[0]
    own = run([(q_ref[...], aux_ref[...], float(HOPS * cells), 1.0)])
    sums[2 * HOPS, :, :] = own[0]
    stats[2 * HOPS, 0:1, :] = own[1]
    stats[2 * HOPS, 1:2, :] = own[2]

    def pair(k, _):
        parts = []
        for j, sign in ((0, 1), (1, -1)):
            i = 2 * k + j
            for source, target, send, recv in (
                (q_ref, q_got, q_send, q_recv),
                (aux_ref, aux_got, a_send, a_recv),
            ):
                pltpu.make_async_remote_copy(
                    src_ref=source, dst_ref=target.at[i], send_sem=send.at[i], recv_sem=recv.at[i],
                    device_id=device(1), device_id_type=MESH,
                ).wait_recv()
            slot = HOPS + sign * (k + 1)
            parts.append((q_got[i], aux_got[i], (slot * cells).astype(jnp.float32), 1.0))
        summed, peak, total = run(parts)
        for j, sign in ((0, 1), (1, -1)):
            i = 2 * k + j
            lanes = slice(j * rows, (j + 1) * rows)
            sums[i, :, :] = summed[:, lanes]
            stats[i, 0:1, :] = peak[:, lanes]
            stats[i, 1:2, :] = total[:, lanes]
            for source, target, send, recv in (
                (sums, sums_got, o_send, o_recv),
                (stats, stats_got, t_send, t_recv),
            ):
                pltpu.make_async_remote_copy(
                    src_ref=source.at[i], dst_ref=target.at[i],
                    send_sem=send.at[i], recv_sem=recv.at[i],
                    device_id=device(-sign * (k + 1)), device_id_type=MESH,
                ).start()
        return 0

    lax.fori_loop(0, HOPS, pair, 0)

    for i in range(2 * HOPS):
        for source, target, send, recv in (
            (sums, sums_got, o_send, o_recv),
            (stats, stats_got, t_send, t_recv),
        ):
            copy = pltpu.make_async_remote_copy(
                src_ref=source.at[i], dst_ref=target.at[i],
                send_sem=send.at[i], recv_sem=recv.at[i],
                device_id=device(1), device_id_type=MESH,
            )
            copy.wait_recv()
            copy.wait_send()

    for copy in sent:
        copy.wait_send()

    peak = stats[2 * HOPS, 0:1, :]
    for i in range(2 * HOPS):
        peak = jnp.maximum(peak, stats_got[i, 0:1, :])
    factors = [jnp.exp2(stats[2 * HOPS, 0:1, :] - peak)]
    total = stats[2 * HOPS, 1:2, :] * factors[0]
    for i in range(2 * HOPS):
        factors.append(jnp.exp2(stats_got[i, 0:1, :] - peak))
        total += stats_got[i, 1:2, :] * factors[i + 1]
    width = sums.shape[1]
    for c in range(0, width, 128):
        piece = sums[2 * HOPS, c : c + 128, :] * factors[0]
        for i in range(2 * HOPS):
            piece += sums_got[i, c : c + 128, :] * factors[i + 1]
        out_ref[:, c : c + 128] = (piece / total).T


def line_kernel(
    size,
    q_ref, q_rope_ref, home_ref, length_ref, cache_hbm, rope_ref, out_ref,
    kcat, vt_hi, vt_lo, s_ref, ph_ref, pl_ref,
    cache, q_all, aux_all, acc, got, fac,
    fetch_sem, own_sem, q_send, q_recv, r_send, r_recv,
):
    me = lax.axis_index("blk")
    count = size // 2
    z, y = me // 2, lax.rem(me, 2)
    far = z >= count // 2
    end = (z == 0) | (z == count - 1)
    inward = jnp.where(far, -1, 1)
    cells, width = cache.shape
    rows = q_ref.shape[0]
    window = (2 * HOPS + 1) * cells
    tall = rows // PIECES
    met = links_used(count)
    ways = sorted({link for links in met.values() for link in links})
    devices = {
        link: {
            "blk": 2 * jnp.clip(z + link[0] * inward, 0, count - 1) + (1 - y if link[1] else y)
        }
        for link in ways
    }

    def remote(source, target, send, recv, link):
        return pltpu.make_async_remote_copy(
            src_ref=source, dst_ref=target, send_sem=send, recv_sem=recv,
            device_id=devices[link], device_id_type=MESH,
        )

    def q_part(slot, p):
        if p == PIECES:
            return aux_all.at[slot]
        return q_all.at[slot, pl.ds(p * tall, tall)]

    def q_copy(kind, link, slot, p):
        there = landing(count, kind, link, slot)
        return remote(
            q_part(slot, p), q_part(there, p), q_send.at[ways.index(link), slot, p], q_recv.at[there, p], link
        )

    def parts_of(p):
        return (PIECES, 0) if p == 0 else (p,)

    def q_start(kind, link, slot, p):
        for part in parts_of(p):
            q_copy(kind, link, slot, part).start()

    def q_wait(slot, p):
        for part in parts_of(p):
            piece = q_part(slot, part)
            remote(piece, piece, q_send.at[0, slot, part], q_recv.at[slot, part], Y).wait_recv()

    def r_part(ref, k):
        return ref.at[pl.ds(0, 8 + deep)] if k == 0 else ref.at[pl.ds(8 + k * deep, deep)]

    deep = width // PARTS

    sides = list(range(size))

    def r_copy(kind, link, slot, k):
        there = landing(count, kind, link, slot)
        side = sides.index(landing(count, kind, link, 2 * kind))
        return remote(
            r_part(acc.at[slot], k), r_part(got.at[side, there], k),
            r_send.at[slot, k], r_recv.at[side, there, k], link,
        )

    def merge(slot, side, k):
        piece = r_part(got.at[side, slot], k)
        remote(piece, piece, r_send.at[slot, k], r_recv.at[side, slot, k], Y).wait_recv()
        if k == 0:
            first, second = acc[slot, 0:1, :], got[side, slot, 0:1, :]
            peak = jnp.maximum(first, second)
            first, second = jnp.exp2(first - peak), jnp.exp2(second - peak)
            total = acc[slot, 1:2, :] * first + got[side, slot, 1:2, :] * second
            acc[slot, 0:1, :] = peak
            acc[slot, 1:2, :] = total
            fac[side, slot, 0:1, :] = first
            fac[side, slot, 1:2, :] = second
        else:
            first, second = fac[side, slot, 0:1, :], fac[side, slot, 1:2, :]
        lines = slice(8 + k * deep, 8 + (k + 1) * deep)
        acc[slot, lines, :] = acc[slot, lines, :] * first + got[side, slot, lines, :] * second

    sent_q, sent_r = {END: [], MID: []}, {END: [], MID: []}

    def perform(kind, actions, note):
        for action, slot, source, pieces, link in actions:
            for p in pieces:
                if action == TAKE:
                    q_wait(slot, p)
                if action == JOIN:
                    merge(slot, source, p)
                for way in link if action == TAKE else () if link is None else (link,):
                    if action in (SEND, TAKE):
                        q_start(kind, way, slot, p)
                        note[0].extend((way, slot, part) for part in parts_of(p))
                    else:
                        r_copy(kind, way, slot, p).start()
                        note[1].append((way, slot, p))

    kinds = ((END, end), (MID, jnp.logical_not(end)))

    def run(point, stages, visit=None):
        for kind, here in kinds:
            due = [(k, PLAN[kind, k, point]) for k in stages if (kind, k, point) in PLAN]
            if due:

                @pl.when(here)
                def _(kind=kind, due=due):
                    for k, actions in due:
                        note = (sent_q[kind], sent_r[kind])
                        if visit is None:
                            perform(kind, actions, note)
                        else:
                            pl.when(visit == k)(
                                functools.partial(perform, kind, actions, note)
                            )

    mine = jnp.where(end, 0, 2)
    own_copy = pltpu.make_async_copy(q_ref, q_all.at[mine], own_sem.at[0])
    own_copy.start()

    def fetch(i):
        part = pl.ds(pl.multiple_of(i * STEP, STEP), STEP)
        return pltpu.make_async_copy(cache_hbm.at[part], cache.at[part], fetch_sem.at[i])

    for i in range(cells // STEP):
        fetch(i).start()

    barrier = pltpu.get_barrier_semaphore()
    for kind, here in kinds:

        @pl.when(here)
        def _(kind=kind):
            for link in met[kind]:
                pl.semaphore_signal(
                    barrier, inc=1, device_id=devices[link], device_id_type=MESH
                )

    height, heads, _ = q_rope_ref.shape
    packed = jnp.concatenate([q_rope_ref[i] for i in range(height)], axis=1)
    aux_all[mine, 0:heads, :] = packed
    line = lax.broadcasted_iota(jnp.int32, (8, rows), 0)
    lane = lax.broadcasted_iota(jnp.int32, (8, rows), 1)
    meta = jnp.zeros((8, rows), jnp.float32)
    for i in range(height):
        values = jnp.where(
            line == 0, home_ref[i].astype(jnp.float32), length_ref[i].astype(jnp.float32)
        )
        meta = jnp.where((lane >= i * heads) & (line < 2), values, meta)
    aux_all[mine, heads : heads + 8, :] = meta

    prepare = functools.partial(prepare_cache, cache, rope_ref, kcat, vt_hi, vt_lo, fetch)
    prepare(0, BEFORE)
    own_copy.wait()
    pl.semaphore_wait(barrier, jnp.where(end, len(met[END]), len(met[MID])))
    run(0, (START,))
    prepare(BEFORE, cells // STEP)

    def pick(i, c):
        chosen = jnp.int32(0)
        for kind, here in kinds:
            for k, pair in enumerate(ORDER[kind]):
                chosen = jnp.where(here & (i == k), pair[c], chosen)
        return chosen

    def step(i, _):
        def hook(point):
            run(point, range(len(ORDER[END])), i)

        hook(0)
        parts, slots = [], []
        for c in range(2):
            slot = pick(i, c)
            label = slot // 2
            block = 2 * jnp.where(far, count - 1 - label, label)
            block += jnp.where(lax.rem(slot, 2) == 0, y, 1 - y)
            place = lax.rem(me - block + HOPS + size, size)
            parts.append((q_all[slot], aux_all[slot], (place * cells).astype(jnp.float32)))
            slots.append(slot)
        visit_line(parts, kcat, vt_hi, vt_lo, s_ref, ph_ref, pl_ref, window, acc, slots, hook)
        return 0

    lax.fori_loop(0, len(ORDER[END]), step, 0)
    run(0, (REST,))

    def result(own):
        total = acc[own, 1:2, :]
        for c in range(0, width, 128):
            out_ref[:, c : c + 128] = (acc[own, 8 + c : 8 + c + 128, :] / total).T

    for kind, here in kinds:

        @pl.when(here)
        def _(kind=kind):
            result(0 if kind == END else 2)
            for link, slot, part in sent_q[kind]:
                q_copy(kind, link, slot, part).wait_send()
            for link, slot, k in sent_r[kind]:
                r_copy(kind, link, slot, k).wait_send()


def visit_line(parts, kcat, vt_hi, vt_lo, s_ref, ph_ref, pl_ref, window, acc, slots, hook):
    cells = kcat.shape[0]
    width = vt_hi.shape[0]
    heads = parts[0][1].shape[0] - 8
    query = jnp.concatenate([p[0] for p in parts], axis=0) * FACTOR
    q_hi, q_lo = split(query)
    rope = jnp.concatenate([rope_rows(p[1], heads) for p in parts], axis=0)
    q_cat = jnp.concatenate([q_hi, q_hi, rope], axis=1)
    starts = jnp.concatenate([p[1][heads : heads + 1, :] - p[2] for p in parts], axis=1)
    extents = jnp.concatenate([p[1][heads + 1 : heads + 2, :] for p in parts], axis=1)
    ends = starts + extents
    wrapped = ends - window
    count = query.shape[0]
    rows = count // 2
    peak = jnp.full((1, count), FLOOR, jnp.float32)
    chunks = cells // LONG
    for c in range(chunks):
        lines = slice(c * LONG, (c + 1) * LONG)
        scores = lax.dot_general(kcat[lines, :], q_cat, NT, preferred_element_type=jnp.float32)
        scores += lax.dot_general(
            kcat[lines, 0:width], q_lo, NT, preferred_element_type=jnp.float32
        )
        cell = lax.broadcasted_iota(jnp.int32, (LONG, count), 0).astype(jnp.float32) + c * LONG
        live = ((cell >= starts) & (cell < ends)) | (cell < wrapped)
        scores = jnp.where(live, scores, DEAD)
        s_ref[lines, :] = scores
        peak = jnp.maximum(peak, jnp.max(scores, axis=0, keepdims=True))
    hook(1)
    total = jnp.zeros((1, count), jnp.float32)
    for c in range(chunks):
        lines = slice(c * LONG, (c + 1) * LONG)
        weights = jnp.exp2(s_ref[lines, :] - peak)
        total += jnp.sum(weights, axis=0, keepdims=True)
        high, low = split(weights)
        ph_ref[lines, :] = high
        pl_ref[lines, :] = low
    for j, slot in enumerate(slots):
        lanes = slice(j * rows, (j + 1) * rows)
        acc[slot, 0:1, :] = peak[:, lanes]
        acc[slot, 1:2, :] = total[:, lanes]
    hook(2)
    turn = width // TURNS
    for h in range(TURNS):
        feats = slice(h * turn, (h + 1) * turn)
        summed = jnp.dot(vt_hi[feats, :], ph_ref[...], preferred_element_type=jnp.float32)
        summed += jnp.dot(vt_hi[feats, :], pl_ref[...], preferred_element_type=jnp.float32)
        summed += jnp.dot(vt_lo[feats, :], ph_ref[...], preferred_element_type=jnp.float32)
        for j, slot in enumerate(slots):
            lanes = slice(j * rows, (j + 1) * rows)
            acc[slot, 8 + h * turn : 8 + (h + 1) * turn, :] = summed[:, lanes]
        hook(3 + h)


def pack_aux(q_rope, home_offset, lengths):
    height, heads, rope = q_rope.shape
    packed = jnp.concatenate([q_rope[i] for i in range(height)], axis=1)
    meta = jnp.stack([home_offset, lengths]).astype(jnp.float32)
    meta = jnp.repeat(meta, heads, axis=1)
    return jnp.concatenate([packed, meta, jnp.zeros((6, height * heads), jnp.float32)], axis=0)


def shards(size, q_latent, q_rope, cache_latent, cache_rope, home_offset, lengths):
    height, heads, width = q_latent.shape
    cells, rope = cache_rope.shape
    rows = height * heads
    flat = q_latent.reshape(rows, width)
    rope_turned = cache_rope.T
    dma = pltpu.SemaphoreType.DMA
    vmem, anywhere = (pl.BlockSpec(memory_space=m) for m in (pltpu.VMEM, pl.ANY))
    working = [
        pltpu.VMEM((cells, 2 * width + 4 * rope), jnp.bfloat16),
        pltpu.VMEM((width, cells), jnp.bfloat16),
        pltpu.VMEM((width, cells), jnp.bfloat16),
        pltpu.VMEM((cells, 2 * rows), jnp.float32),
        pltpu.VMEM((cells, 2 * rows), jnp.bfloat16),
        pltpu.VMEM((cells, 2 * rows), jnp.bfloat16),
    ]
    if size == 2 * HOPS + 2:
        kernel = line_kernel
        smem = pl.BlockSpec(memory_space=pltpu.SMEM)
        in_specs = [anywhere, vmem, smem, smem, anywhere, vmem]
        operands = (flat, q_rope, home_offset, lengths, cache_latent, rope_turned)
        ways = {link for links in links_used(size // 2).values() for link in links}
        scratch = [
            pltpu.VMEM((cells, width), jnp.float32),
            pltpu.VMEM((size, rows, width), jnp.float32),
            pltpu.VMEM((size, heads + 8, rows), jnp.float32),
            pltpu.VMEM((size, width + 8, rows), jnp.float32),
            pltpu.VMEM((size, size, width + 8, rows), jnp.float32),
            pltpu.VMEM((size, size, 8, rows), jnp.float32),
            dma((cells // STEP,)),
            dma((1,)),
            dma((len(ways), size, PIECES + 1)),
            dma((size, PIECES + 1)),
            dma((size, PARTS)),
            dma((size, size, PARTS)),
        ]
    else:
        kernel = window_kernel
        n = 2 * HOPS
        in_specs = [vmem] * 4
        operands = (flat, pack_aux(q_rope, home_offset, lengths), cache_latent, rope_turned)
        scratch = [
            pltpu.VMEM((n, rows, width), jnp.float32),
            pltpu.VMEM((n, heads + 8, rows), jnp.float32),
            pltpu.VMEM((n + 1, width, rows), jnp.float32),
            pltpu.VMEM((n + 1, 8, rows), jnp.float32),
            pltpu.VMEM((n, width, rows), jnp.float32),
            pltpu.VMEM((n, 8, rows), jnp.float32),
        ] + [dma((n,))] * 8
    out = pl.pallas_call(
        functools.partial(kernel, size),
        out_shape=jax.ShapeDtypeStruct((rows, width), jnp.float32),
        in_specs=in_specs,
        out_specs=vmem,
        scratch_shapes=working + scratch,
        compiler_params=pltpu.CompilerParams(
            collective_id=0, has_side_effects=True, vmem_limit_bytes=60 * 1024 * 1024
        ),
    )(*operands)
    return out.reshape(height, heads, width)


def solution(mesh):
    return jax.shard_map(
        functools.partial(shards, mesh.shape["blk"]),
        mesh=mesh,
        in_specs=(
            P(("groups", "blk"), "head", None),
            P(("groups", "blk"), "head", None),
            P(("groups", "blk"), None),
            P(("groups", "blk"), None),
            P(("groups", "blk")),
            P(("groups", "blk")),
        ),
        out_specs=P(("groups", "blk"), "head", None),
        check_vma=False,
    )
```

```python
import functools
import math

import jax
import jax.numpy as jnp
from jax import lax
from jax.experimental import pallas as pl
from jax.experimental.pallas import tpu as pltpu
from jax.sharding import PartitionSpec as P

ROPE = 64
NOPE = 128
HOPS = 3

MESH = pl.DeviceIdType.MESH
FLOOR = -1e30
DEAD = -2e30
FACTOR = math.log2(math.e) / math.sqrt(NOPE + ROPE)
CHUNK = 256
LONG = 512
STEP = 256

NT = (((1,), (1,)), ((), ()))

Y, IN, OUT, OVER, CROSS, FAR = (0, 1), (1, 0), (-1, 0), (2, 0), (2, 1), (3, 0)
END, MID = 0, 1
START, REST = -1, 9
SEND, TAKE, GIVE, JOIN = range(4)
PIECES = 4
PARTS = 4
TURNS = 2
BEFORE = 2
ORDER = {
    END: ((0, 0), (1, 6), (5, 7), (3, 2)),
    MID: ((4, 5), (0, 1), (7, 3), (2, 2)),
}
PLAN = {
    (END, START, 0): (
        (SEND, 0, 0, (1,), Y),
        (SEND, 0, 0, (0,), Y),
        (SEND, 0, 0, (2,), IN),
        (SEND, 0, 0, (3,), Y),
        (SEND, 0, 0, (1,), IN),
        (SEND, 0, 0, (3,), IN),
        (SEND, 0, 0, (2,), Y),
        (SEND, 0, 0, (0,), IN),
    ),
    (END, 0, 2): (
        (TAKE, 2, 0, (0,), (Y,)),
    ),
    (END, 0, 4): (
        (TAKE, 2, 0, (1, 2, 3,), (Y,)),
    ),
    (END, 1, 0): (
        (TAKE, 6, 0, (0, 1, 2, 3,), (Y,)),
        (TAKE, 1, 0, (0, 1, 2, 3,), ()),
    ),
    (END, 1, 4): (
        (GIVE, 1, 0, (0, 1, 2, 3,), Y),
        (GIVE, 6, 0, (0, 1, 2, 3,), Y),
    ),
    (END, 2, 0): (
        (TAKE, 5, 0, (0, 1, 2, 3,), ()),
        (TAKE, 7, 0, (0, 1, 2, 3,), ()),
    ),
    (END, 2, 4): (
        (GIVE, 5, 0, (0, 1, 2, 3,), CROSS),
    ),
    (END, 3, 0): (
        (TAKE, 3, 0, (0, 1, 2, 3,), ()),
    ),
    (END, 3, 4): (
        (GIVE, 3, 0, (0, 1, 2, 3,), Y),
        (JOIN, 7, 1, (0, 1,), IN),
        (JOIN, 0, 2, (0,), None),
    ),
    (END, REST, 0): (
        (JOIN, 7, 1, (2,), IN),
        (JOIN, 0, 2, (1,), None),
        (JOIN, 0, 1, (0, 1,), None),
        (JOIN, 7, 1, (3,), IN),
        (JOIN, 0, 2, (2,), None),
        (JOIN, 2, 1, (0,), IN),
        (JOIN, 0, 2, (3,), None),
        (JOIN, 0, 1, (2, 3,), None),
        (JOIN, 2, 1, (1, 2, 3,), IN),
        (JOIN, 0, 5, (0, 1, 2, 3,), None),
    ),
    (MID, START, 0): (
        (SEND, 2, 0, (1,), Y),
        (SEND, 2, 0, (3,), OUT),
        (SEND, 2, 0, (0,), IN),
        (SEND, 2, 0, (3,), Y),
        (SEND, 2, 0, (1,), IN),
        (SEND, 2, 0, (0, 1,), OUT),
        (SEND, 2, 0, (2,), IN),
        (SEND, 2, 0, (2,), Y),
        (SEND, 2, 0, (2,), OUT),
        (SEND, 2, 0, (3,), IN),
    ),
    (MID, 0, 0): (
        (TAKE, 4, 0, (0, 1, 2, 3,), (Y,)),
        (TAKE, 0, 0, (0, 1, 2, 3,), (Y, OVER,)),
        (TAKE, 5, 0, (0, 1, 2, 3,), (OUT,)),
    ),
    (MID, 0, 2): (
        (SEND, 2, 0, (0,), Y),
        (TAKE, 1, 0, (0,), (IN,)),
    ),
    (MID, 0, 4): (
        (GIVE, 5, 0, (0, 1, 2, 3,), Y),
        (TAKE, 1, 0, (1, 2,), (IN,)),
    ),
    (MID, 1, 0): (
        (TAKE, 1, 0, (3,), (IN,)),
    ),
    (MID, 1, 4): (
        (GIVE, 1, 0, (0, 1, 2, 3,), Y),
        (JOIN, 4, 3, (0, 1,), IN),
    ),
    (MID, 2, 0): (
        (JOIN, 4, 3, (2,), IN),
        (TAKE, 3, 0, (0, 1, 2, 3,), ()),
        (TAKE, 7, 0, (0, 1, 2, 3,), ()),
    ),
    (MID, 2, 2): (
        (JOIN, 4, 3, (3,), IN),
        (JOIN, 0, 3, (0, 1,), OUT),
    ),
    (MID, 2, 4): (
        (GIVE, 3, 0, (0, 1, 2, 3,), Y),
        (JOIN, 0, 3, (2, 3,), OUT),
    ),
    (MID, REST, 0): (
        (JOIN, 7, 0, (0,), CROSS),
        (JOIN, 2, 3, (0,), None),
        (JOIN, 2, 4, (0,), None),
        (JOIN, 2, 7, (0,), None),
        (JOIN, 7, 0, (1,), CROSS),
        (JOIN, 2, 3, (1,), None),
        (JOIN, 2, 4, (1,), None),
        (JOIN, 2, 7, (1,), None),
        (JOIN, 7, 0, (2,), CROSS),
        (JOIN, 2, 3, (2,), None),
        (JOIN, 2, 4, (2,), None),
        (JOIN, 2, 7, (2,), None),
        (JOIN, 7, 0, (3,), CROSS),
        (JOIN, 2, 3, (3,), None),
        (JOIN, 2, 4, (3,), None),
        (JOIN, 2, 7, (3,), None),
        (JOIN, 2, 0, (0, 1, 2, 3,), None),
    ),
}


def landing(count, kind, link, slot):
    label, column = divmod(slot, 2)
    if kind + link[0] >= count // 2:
        label = count - 1 - label
    return 2 * label + (column + link[1]) % 2


def links_used(count):
    sent = {
        kind: {
            way
            for (k, _, _), actions in PLAN.items()
            for action, _, _, _, ways in actions
            for way in (ways if action == TAKE else (ways,))
            if k == kind and way is not None
        }
        for kind in (END, MID)
    }
    met = {kind: set(links) for kind, links in sent.items()}
    for kind, links in sent.items():
        for link in links:
            label = kind + link[0]
            label = count - 1 - label if label >= count // 2 else label
            source = landing(count, kind, link, 2 * kind) // 2
            met[label].add((source - label, link[1]))
    return {kind: sorted(links) for kind, links in met.items()}


def split(x):
    high = x.astype(jnp.bfloat16)
    low = (x - high.astype(jnp.float32)).astype(jnp.bfloat16)
    return high, low


def prepare_cache(cache_ref, rope_ref, kcat, vt_hi, vt_lo, fetch=None, first=0, last=None):
    cells, width = cache_ref.shape
    step = STEP

    def body(i, _):
        if fetch is not None:
            fetch(i).wait()
        rows = pl.ds(pl.multiple_of(i * step, step), step)
        block = cache_ref[rows, :]
        high, low = split(block)
        kcat[rows, 0:width] = high
        kcat[rows, width : 2 * width] = low
        turned = block.T
        t_high, t_low = split(turned)
        vt_hi[:, rows] = t_high
        vt_lo[:, rows] = t_low
        rope = rope_ref[:, rows].T
        r_high = rope.astype(jnp.bfloat16).astype(jnp.float32)
        r_low = rope - r_high
        wide = jnp.concatenate([r_high, r_high, r_low, jnp.zeros_like(rope)], axis=1)
        kcat[rows, 2 * width : 2 * width + 4 * rope.shape[1]] = wide.astype(jnp.bfloat16)
        return 0

    lax.fori_loop(first, cells // step if last is None else last, body, 0)


def rope_rows(aux, heads):
    packed = aux[0:heads, :] * FACTOR
    high = packed.astype(jnp.bfloat16).astype(jnp.float32)
    low = packed - high
    half = packed.shape[1] // 2
    blank = jnp.zeros((heads, half), jnp.float32)
    rows = []
    for part in (slice(0, half), slice(half, 2 * half)):
        rows.append(jnp.concatenate([high[:, part], low[:, part], high[:, part], blank], axis=1))
    return jnp.concatenate(rows, axis=0).astype(jnp.bfloat16)


def visit(parts, kcat, vt_hi, vt_lo, s_ref, ph_ref, pl_ref, window):
    cells = kcat.shape[0]
    width = vt_hi.shape[0]
    heads = parts[0][1].shape[0] - 8
    query = jnp.concatenate([p[0] for p in parts], axis=0) * FACTOR
    q_hi, q_lo = split(query)
    rope = jnp.concatenate([rope_rows(p[1], heads) for p in parts], axis=0)
    q_cat = jnp.concatenate([q_hi, q_hi, rope], axis=1)
    starts = jnp.concatenate([p[1][heads : heads + 1, :] - p[2] for p in parts], axis=1)
    extents = jnp.concatenate([p[1][heads + 1 : heads + 2, :] * p[3] for p in parts], axis=1)
    ends = starts + extents
    wrapped = ends - window
    count = query.shape[0]
    peak = jnp.full((1, count), FLOOR, jnp.float32)
    for c in range(cells // CHUNK):
        rows = slice(c * CHUNK, (c + 1) * CHUNK)
        scores = lax.dot_general(kcat[rows, :], q_cat, NT, preferred_element_type=jnp.float32)
        scores += lax.dot_general(
            kcat[rows, 0:width], q_lo, NT, preferred_element_type=jnp.float32
        )
        cell = lax.broadcasted_iota(jnp.int32, (CHUNK, count), 0).astype(jnp.float32) + c * CHUNK
        live = ((cell >= starts) & (cell < ends)) | (cell < wrapped)
        scores = jnp.where(live, scores, DEAD)
        s_ref[rows, 0:count] = scores
        peak = jnp.maximum(peak, jnp.max(scores, axis=0, keepdims=True))
    total = jnp.zeros((1, count), jnp.float32)
    summed = None
    for c in range(cells // CHUNK):
        rows = slice(c * CHUNK, (c + 1) * CHUNK)
        weights = jnp.exp2(s_ref[rows, 0:count] - peak)
        total += jnp.sum(weights, axis=0, keepdims=True)
        high, low = split(weights)
        ph_ref[rows, 0:count] = high
        pl_ref[rows, 0:count] = low
    high = ph_ref[:, 0:count]
    summed = jnp.dot(vt_hi[...], high, preferred_element_type=jnp.float32)
    summed += jnp.dot(vt_hi[...], pl_ref[:, 0:count], preferred_element_type=jnp.float32)
    summed += jnp.dot(vt_lo[...], high, preferred_element_type=jnp.float32)
    return summed, peak, total


def window_kernel(
    size,
    q_ref, aux_ref, cache_ref, rope_ref, out_ref,
    kcat, vt_hi, vt_lo, s_ref, ph_ref, pl_ref,
    q_got, aux_got, sums, stats, sums_got, stats_got,
    q_send, q_recv, a_send, a_recv, o_send, o_recv, t_send, t_recv,
):
    me = lax.axis_index("blk")
    cells = cache_ref.shape[0]
    window = (2 * HOPS + 1) * cells
    distances = [sign * k for k in range(1, HOPS + 1) for sign in (1, -1)]

    def device(distance):
        return {"blk": lax.rem(me + distance + size, size)}

    barrier = pltpu.get_barrier_semaphore()
    for d in distances:
        pl.semaphore_signal(barrier, inc=1, device_id=device(d), device_id_type=MESH)
    pl.semaphore_wait(barrier, 2 * HOPS)

    sent = []
    for i, d in enumerate(distances):
        for source, target, send, recv in (
            (q_ref, q_got, q_send, q_recv),
            (aux_ref, aux_got, a_send, a_recv),
        ):
            copy = pltpu.make_async_remote_copy(
                src_ref=source, dst_ref=target.at[i], send_sem=send.at[i], recv_sem=recv.at[i],
                device_id=device(d), device_id_type=MESH,
            )
            copy.start()
            sent.append(copy)

    prepare_cache(cache_ref, rope_ref, kcat, vt_hi, vt_lo)
    run = functools.partial(
        visit, kcat=kcat, vt_hi=vt_hi, vt_lo=vt_lo, s_ref=s_ref, ph_ref=ph_ref, pl_ref=pl_ref,
        window=window,
    )
    rows = q_ref.shape[0]
    own = run([(q_ref[...], aux_ref[...], float(HOPS * cells), 1.0)])
    sums[2 * HOPS, :, :] = own[0]
    stats[2 * HOPS, 0:1, :] = own[1]
    stats[2 * HOPS, 1:2, :] = own[2]

    def pair(k, _):
        parts = []
        for j, sign in ((0, 1), (1, -1)):
            i = 2 * k + j
            for source, target, send, recv in (
                (q_ref, q_got, q_send, q_recv),
                (aux_ref, aux_got, a_send, a_recv),
            ):
                pltpu.make_async_remote_copy(
                    src_ref=source, dst_ref=target.at[i], send_sem=send.at[i], recv_sem=recv.at[i],
                    device_id=device(1), device_id_type=MESH,
                ).wait_recv()
            slot = HOPS + sign * (k + 1)
            parts.append((q_got[i], aux_got[i], (slot * cells).astype(jnp.float32), 1.0))
        summed, peak, total = run(parts)
        for j, sign in ((0, 1), (1, -1)):
            i = 2 * k + j
            lanes = slice(j * rows, (j + 1) * rows)
            sums[i, :, :] = summed[:, lanes]
            stats[i, 0:1, :] = peak[:, lanes]
            stats[i, 1:2, :] = total[:, lanes]
            for source, target, send, recv in (
                (sums, sums_got, o_send, o_recv),
                (stats, stats_got, t_send, t_recv),
            ):
                pltpu.make_async_remote_copy(
                    src_ref=source.at[i], dst_ref=target.at[i],
                    send_sem=send.at[i], recv_sem=recv.at[i],
                    device_id=device(-sign * (k + 1)), device_id_type=MESH,
                ).start()
        return 0

    lax.fori_loop(0, HOPS, pair, 0)

    for i in range(2 * HOPS):
        for source, target, send, recv in (
            (sums, sums_got, o_send, o_recv),
            (stats, stats_got, t_send, t_recv),
        ):
            copy = pltpu.make_async_remote_copy(
                src_ref=source.at[i], dst_ref=target.at[i],
                send_sem=send.at[i], recv_sem=recv.at[i],
                device_id=device(1), device_id_type=MESH,
            )
            copy.wait_recv()
            copy.wait_send()

    for copy in sent:
        copy.wait_send()

    peak = stats[2 * HOPS, 0:1, :]
    for i in range(2 * HOPS):
        peak = jnp.maximum(peak, stats_got[i, 0:1, :])
    factors = [jnp.exp2(stats[2 * HOPS, 0:1, :] - peak)]
    total = stats[2 * HOPS, 1:2, :] * factors[0]
    for i in range(2 * HOPS):
        factors.append(jnp.exp2(stats_got[i, 0:1, :] - peak))
        total += stats_got[i, 1:2, :] * factors[i + 1]
    width = sums.shape[1]
    for c in range(0, width, 128):
        piece = sums[2 * HOPS, c : c + 128, :] * factors[0]
        for i in range(2 * HOPS):
            piece += sums_got[i, c : c + 128, :] * factors[i + 1]
        out_ref[:, c : c + 128] = (piece / total).T


def line_kernel(
    size,
    q_ref, q_rope_ref, home_ref, length_ref, cache_hbm, rope_ref, out_ref,
    kcat, vt_hi, vt_lo, s_ref, ph_ref, pl_ref,
    cache, q_all, aux_all, acc, got, fac,
    fetch_sem, own_sem, q_send, q_recv, r_send, r_recv,
):
    me = lax.axis_index("blk")
    count = size // 2
    z, y = me // 2, lax.rem(me, 2)
    far = z >= count // 2
    end = (z == 0) | (z == count - 1)
    inward = jnp.where(far, -1, 1)
    cells, width = cache.shape
    rows = q_ref.shape[0]
    window = (2 * HOPS + 1) * cells
    tall = rows // PIECES
    met = links_used(count)
    ways = sorted({link for links in met.values() for link in links})
    devices = {
        link: {
            "blk": 2 * jnp.clip(z + link[0] * inward, 0, count - 1) + (1 - y if link[1] else y)
        }
        for link in ways
    }

    def remote(source, target, send, recv, link):
        return pltpu.make_async_remote_copy(
            src_ref=source, dst_ref=target, send_sem=send, recv_sem=recv,
            device_id=devices[link], device_id_type=MESH,
        )

    def q_part(slot, p):
        if p == PIECES:
            return aux_all.at[slot]
        return q_all.at[slot, pl.ds(p * tall, tall)]

    def q_copy(kind, link, slot, p):
        there = landing(count, kind, link, slot)
        return remote(
            q_part(slot, p), q_part(there, p), q_send.at[ways.index(link), slot, p], q_recv.at[there, p], link
        )

    def parts_of(p):
        return (PIECES, 0) if p == 0 else (p,)

    def q_start(kind, link, slot, p):
        for part in parts_of(p):
            q_copy(kind, link, slot, part).start()

    def q_wait(slot, p):
        for part in parts_of(p):
            piece = q_part(slot, part)
            remote(piece, piece, q_send.at[0, slot, part], q_recv.at[slot, part], Y).wait_recv()

    def r_part(ref, k):
        return ref.at[pl.ds(0, 8 + deep)] if k == 0 else ref.at[pl.ds(8 + k * deep, deep)]

    deep = width // PARTS

    sides = list(range(size))

    def r_copy(kind, link, slot, k):
        there = landing(count, kind, link, slot)
        side = sides.index(landing(count, kind, link, 2 * kind))
        return remote(
            r_part(acc.at[slot], k), r_part(got.at[side, there], k),
            r_send.at[slot, k], r_recv.at[side, there, k], link,
        )

    def merge(slot, side, k):
        piece = r_part(got.at[side, slot], k)
        remote(piece, piece, r_send.at[slot, k], r_recv.at[side, slot, k], Y).wait_recv()
        if k == 0:
            first, second = acc[slot, 0:1, :], got[side, slot, 0:1, :]
            peak = jnp.maximum(first, second)
            first, second = jnp.exp2(first - peak), jnp.exp2(second - peak)
            total = acc[slot, 1:2, :] * first + got[side, slot, 1:2, :] * second
            acc[slot, 0:1, :] = peak
            acc[slot, 1:2, :] = total
            fac[side, slot, 0:1, :] = first
            fac[side, slot, 1:2, :] = second
        else:
            first, second = fac[side, slot, 0:1, :], fac[side, slot, 1:2, :]
        lines = slice(8 + k * deep, 8 + (k + 1) * deep)
        acc[slot, lines, :] = acc[slot, lines, :] * first + got[side, slot, lines, :] * second

    sent_q, sent_r = {END: [], MID: []}, {END: [], MID: []}

    def perform(kind, actions, note):
        for action, slot, source, pieces, link in actions:
            for p in pieces:
                if action == TAKE:
                    q_wait(slot, p)
                if action == JOIN:
                    merge(slot, source, p)
                for way in link if action == TAKE else () if link is None else (link,):
                    if action in (SEND, TAKE):
                        q_start(kind, way, slot, p)
                        note[0].extend((way, slot, part) for part in parts_of(p))
                    else:
                        r_copy(kind, way, slot, p).start()
                        note[1].append((way, slot, p))

    kinds = ((END, end), (MID, jnp.logical_not(end)))

    def run(point, stages, visit=None):
        for kind, here in kinds:
            due = [(k, PLAN[kind, k, point]) for k in stages if (kind, k, point) in PLAN]
            if due:

                @pl.when(here)
                def _(kind=kind, due=due):
                    for k, actions in due:
                        note = (sent_q[kind], sent_r[kind])
                        if visit is None:
                            perform(kind, actions, note)
                        else:
                            pl.when(visit == k)(
                                functools.partial(perform, kind, actions, note)
                            )

    mine = jnp.where(end, 0, 2)
    own_copy = pltpu.make_async_copy(q_ref, q_all.at[mine], own_sem.at[0])
    own_copy.start()

    def fetch(i):
        part = pl.ds(pl.multiple_of(i * STEP, STEP), STEP)
        return pltpu.make_async_copy(cache_hbm.at[part], cache.at[part], fetch_sem.at[i])

    for i in range(cells // STEP):
        fetch(i).start()

    barrier = pltpu.get_barrier_semaphore()
    for kind, here in kinds:

        @pl.when(here)
        def _(kind=kind):
            for link in met[kind]:
                pl.semaphore_signal(
                    barrier, inc=1, device_id=devices[link], device_id_type=MESH
                )

    height, heads, _ = q_rope_ref.shape
    packed = jnp.concatenate([q_rope_ref[i] for i in range(height)], axis=1)
    aux_all[mine, 0:heads, :] = packed
    line = lax.broadcasted_iota(jnp.int32, (8, rows), 0)
    lane = lax.broadcasted_iota(jnp.int32, (8, rows), 1)
    meta = jnp.zeros((8, rows), jnp.float32)
    for i in range(height):
        values = jnp.where(
            line == 0, home_ref[i].astype(jnp.float32), length_ref[i].astype(jnp.float32)
        )
        meta = jnp.where((lane >= i * heads) & (line < 2), values, meta)
    aux_all[mine, heads : heads + 8, :] = meta

    prepare = functools.partial(prepare_cache, cache, rope_ref, kcat, vt_hi, vt_lo, fetch)
    prepare(0, BEFORE)
    own_copy.wait()
    pl.semaphore_wait(barrier, jnp.where(end, len(met[END]), len(met[MID])))
    run(0, (START,))
    prepare(BEFORE, cells // STEP)

    def pick(i, c):
        chosen = jnp.int32(0)
        for kind, here in kinds:
            for k, pair in enumerate(ORDER[kind]):
                chosen = jnp.where(here & (i == k), pair[c], chosen)
        return chosen

    def step(i, _):
        def hook(point):
            run(point, range(len(ORDER[END])), i)

        hook(0)
        parts, slots = [], []
        for c in range(2):
            slot = pick(i, c)
            label = slot // 2
            block = 2 * jnp.where(far, count - 1 - label, label)
            block += jnp.where(lax.rem(slot, 2) == 0, y, 1 - y)
            place = lax.rem(me - block + HOPS + size, size)
            parts.append((q_all[slot], aux_all[slot], (place * cells).astype(jnp.float32)))
            slots.append(slot)
        visit_line(parts, kcat, vt_hi, vt_lo, s_ref, ph_ref, pl_ref, window, acc, slots, hook)
        return 0

    lax.fori_loop(0, len(ORDER[END]), step, 0)
    run(0, (REST,))

    def result(own):
        total = acc[own, 1:2, :]
        for c in range(0, width, 128):
            out_ref[:, c : c + 128] = (acc[own, 8 + c : 8 + c + 128, :] / total).T

    for kind, here in kinds:

        @pl.when(here)
        def _(kind=kind):
            result(0 if kind == END else 2)
            for link, slot, part in sent_q[kind]:
                q_copy(kind, link, slot, part).wait_send()
            for link, slot, k in sent_r[kind]:
                r_copy(kind, link, slot, k).wait_send()


def visit_line(parts, kcat, vt_hi, vt_lo, s_ref, ph_ref, pl_ref, window, acc, slots, hook):
    cells = kcat.shape[0]
    width = vt_hi.shape[0]
    heads = parts[0][1].shape[0] - 8
    query = jnp.concatenate([p[0] for p in parts], axis=0) * FACTOR
    q_hi, q_lo = split(query)
    rope = jnp.concatenate([rope_rows(p[1], heads) for p in parts], axis=0)
    q_cat = jnp.concatenate([q_hi, q_hi, rope], axis=1)
    starts = jnp.concatenate([p[1][heads : heads + 1, :] - p[2] for p in parts], axis=1)
    extents = jnp.concatenate([p[1][heads + 1 : heads + 2, :] for p in parts], axis=1)
    wrapped = starts + extents - window
    whole = wrapped <= 0
    flip = jnp.where(whole, 1.0, -1.0)
    middle = 0.5 * jnp.where(whole, starts + extents - 1, wrapped - 1) + 0.5 * starts
    bound = 0.5 * jnp.where(whole, extents, extents - window)
    count = query.shape[0]
    rows = count // 2
    peak = jnp.full((8, count), FLOOR, jnp.float32)
    chunks = cells // LONG
    for c in range(chunks):
        lines = slice(c * LONG, (c + 1) * LONG)
        scores = lax.dot_general(kcat[lines, :], q_cat, NT, preferred_element_type=jnp.float32)
        scores += lax.dot_general(
            kcat[lines, 0:width], q_lo, NT, preferred_element_type=jnp.float32
        )
        cell = lax.broadcasted_iota(jnp.int32, (LONG, count), 0).astype(jnp.float32)
        live = jnp.abs(cell - (middle - c * LONG)) * flip < bound
        scores = jnp.where(live, scores, DEAD)
        s_ref[lines, :] = scores
        peak = jnp.maximum(peak, jnp.max(scores.reshape(LONG // 8, 8, count), axis=0))
    peak = jnp.max(peak, axis=0, keepdims=True)
    hook(1)
    total = jnp.zeros((8, count), jnp.float32)
    for c in range(chunks):
        lines = slice(c * LONG, (c + 1) * LONG)
        weights = jnp.exp2(s_ref[lines, :] - peak)
        total += jnp.sum(weights.reshape(LONG // 8, 8, count), axis=0)
        high, low = split(weights)
        ph_ref[lines, :] = high
        pl_ref[lines, :] = low
    total = jnp.sum(total, axis=0, keepdims=True)
    for j, slot in enumerate(slots):
        lanes = slice(j * rows, (j + 1) * rows)
        acc[slot, 0:1, :] = peak[:, lanes]
        acc[slot, 1:2, :] = total[:, lanes]
    hook(2)
    turn = width // TURNS
    for h in range(TURNS):
        feats = slice(h * turn, (h + 1) * turn)
        summed = jnp.dot(vt_hi[feats, :], ph_ref[...], preferred_element_type=jnp.float32)
        summed += jnp.dot(vt_hi[feats, :], pl_ref[...], preferred_element_type=jnp.float32)
        summed += jnp.dot(vt_lo[feats, :], ph_ref[...], preferred_element_type=jnp.float32)
        for j, slot in enumerate(slots):
            lanes = slice(j * rows, (j + 1) * rows)
            acc[slot, 8 + h * turn : 8 + (h + 1) * turn, :] = summed[:, lanes]
        hook(3 + h)


def pack_aux(q_rope, home_offset, lengths):
    height, heads, rope = q_rope.shape
    packed = jnp.concatenate([q_rope[i] for i in range(height)], axis=1)
    meta = jnp.stack([home_offset, lengths]).astype(jnp.float32)
    meta = jnp.repeat(meta, heads, axis=1)
    return jnp.concatenate([packed, meta, jnp.zeros((6, height * heads), jnp.float32)], axis=0)


def shards(size, q_latent, q_rope, cache_latent, cache_rope, home_offset, lengths):
    height, heads, width = q_latent.shape
    cells, rope = cache_rope.shape
    rows = height * heads
    flat = q_latent.reshape(rows, width)
    rope_turned = cache_rope.T
    dma = pltpu.SemaphoreType.DMA
    vmem, anywhere = (pl.BlockSpec(memory_space=m) for m in (pltpu.VMEM, pl.ANY))
    working = [
        pltpu.VMEM((cells, 2 * width + 4 * rope), jnp.bfloat16),
        pltpu.VMEM((width, cells), jnp.bfloat16),
        pltpu.VMEM((width, cells), jnp.bfloat16),
        pltpu.VMEM((cells, 2 * rows), jnp.float32),
        pltpu.VMEM((cells, 2 * rows), jnp.bfloat16),
        pltpu.VMEM((cells, 2 * rows), jnp.bfloat16),
    ]
    if size == 2 * HOPS + 2:
        kernel = line_kernel
        smem = pl.BlockSpec(memory_space=pltpu.SMEM)
        in_specs = [anywhere, vmem, smem, smem, anywhere, vmem]
        operands = (flat, q_rope, home_offset, lengths, cache_latent, rope_turned)
        ways = {link for links in links_used(size // 2).values() for link in links}
        scratch = [
            pltpu.VMEM((cells, width), jnp.float32),
            pltpu.VMEM((size, rows, width), jnp.float32),
            pltpu.VMEM((size, heads + 8, rows), jnp.float32),
            pltpu.VMEM((size, width + 8, rows), jnp.float32),
            pltpu.VMEM((size, size, width + 8, rows), jnp.float32),
            pltpu.VMEM((size, size, 8, rows), jnp.float32),
            dma((cells // STEP,)),
            dma((1,)),
            dma((len(ways), size, PIECES + 1)),
            dma((size, PIECES + 1)),
            dma((size, PARTS)),
            dma((size, size, PARTS)),
        ]
    else:
        kernel = window_kernel
        n = 2 * HOPS
        in_specs = [vmem] * 4
        operands = (flat, pack_aux(q_rope, home_offset, lengths), cache_latent, rope_turned)
        scratch = [
            pltpu.VMEM((n, rows, width), jnp.float32),
            pltpu.VMEM((n, heads + 8, rows), jnp.float32),
            pltpu.VMEM((n + 1, width, rows), jnp.float32),
            pltpu.VMEM((n + 1, 8, rows), jnp.float32),
            pltpu.VMEM((n, width, rows), jnp.float32),
            pltpu.VMEM((n, 8, rows), jnp.float32),
        ] + [dma((n,))] * 8
    out = pl.pallas_call(
        functools.partial(kernel, size),
        out_shape=jax.ShapeDtypeStruct((rows, width), jnp.float32),
        in_specs=in_specs,
        out_specs=vmem,
        scratch_shapes=working + scratch,
        compiler_params=pltpu.CompilerParams(
            collective_id=0, has_side_effects=True, vmem_limit_bytes=60 * 1024 * 1024
        ),
    )(*operands)
    return out.reshape(height, heads, width)


def solution(mesh):
    return jax.shard_map(
        functools.partial(shards, mesh.shape["blk"]),
        mesh=mesh,
        in_specs=(
            P(("groups", "blk"), "head", None),
            P(("groups", "blk"), "head", None),
            P(("groups", "blk"), None),
            P(("groups", "blk"), None),
            P(("groups", "blk")),
            P(("groups", "blk")),
        ),
        out_specs=P(("groups", "blk"), "head", None),
        check_vma=False,
    )
```

```python
import functools
import math

import jax
import jax.numpy as jnp
from jax import lax
from jax.experimental import pallas as pl
from jax.experimental.pallas import tpu as pltpu
from jax.sharding import PartitionSpec as P

ROPE = 64
NOPE = 128
HOPS = 3

MESH = pl.DeviceIdType.MESH
FLOOR = -1e30
DEAD = -2e30
FACTOR = math.log2(math.e) / math.sqrt(NOPE + ROPE)
CHUNK = 256
LONG = 512
STEP = 256

NT = (((1,), (1,)), ((), ()))

Y, IN, OUT, OVER, CROSS, FAR = (0, 1), (1, 0), (-1, 0), (2, 0), (2, 1), (3, 0)
END, MID = 0, 1
START, REST = -1, 9
SEND, TAKE, GIVE, JOIN = range(4)
PIECES = 4
PARTS = 4
TURNS = 2
BEFORE = 2
ORDER = {
    END: ((0, 0), (1, 6), (5, 3), (7, 2)),
    MID: ((2, 2), (5, 4), (0, 1), (3, 7)),
}
PLAN = {
    (END, START, 0): (
        (SEND, 0, 0, (3,), Y),
        (SEND, 0, 0, (1,), Y),
        (SEND, 0, 0, (3,), IN),
        (SEND, 0, 0, (1,), IN),
        (SEND, 0, 0, (0,), Y),
        (SEND, 0, 0, (2,), IN),
        (SEND, 0, 0, (2,), Y),
        (SEND, 0, 0, (0,), IN),
    ),
    (END, 0, 2): (
        (TAKE, 2, 0, (0,), (Y,)),
    ),
    (END, 0, 4): (
        (TAKE, 2, 0, (1,), (Y,)),
    ),
    (END, 1, 0): (
        (TAKE, 2, 0, (2, 3,), (Y,)),
        (TAKE, 6, 0, (0, 1, 2, 3,), (Y,)),
        (TAKE, 1, 0, (0, 1, 2, 3,), ()),
    ),
    (END, 1, 4): (
        (GIVE, 1, 0, (0, 1, 2, 3,), Y),
        (GIVE, 6, 0, (0, 1, 2, 3,), Y),
    ),
    (END, 2, 0): (
        (TAKE, 3, 0, (0, 1, 2, 3,), ()),
        (TAKE, 5, 0, (0, 1, 2, 3,), ()),
    ),
    (END, 2, 4): (
        (GIVE, 3, 0, (0, 1, 2, 3,), Y),
        (GIVE, 5, 0, (0, 1, 2, 3,), CROSS),
    ),
    (END, 3, 0): (
        (TAKE, 7, 0, (0, 1, 2, 3,), ()),
    ),
    (END, 3, 4): (
        (JOIN, 7, 1, (0, 1, 2,), IN),
    ),
    (END, REST, 0): (
        (JOIN, 7, 1, (3,), IN),
        (JOIN, 0, 2, (0,), None),
        (JOIN, 2, 1, (0,), IN),
        (JOIN, 0, 2, (1,), None),
        (JOIN, 0, 1, (0, 1,), None),
        (JOIN, 2, 1, (1,), IN),
        (JOIN, 0, 2, (2,), None),
        (JOIN, 2, 1, (2,), IN),
        (JOIN, 0, 2, (3,), None),
        (JOIN, 0, 1, (2, 3,), None),
        (JOIN, 2, 1, (3,), IN),
        (JOIN, 0, 5, (0, 1, 2, 3,), None),
    ),
    (MID, START, 0): (
        (SEND, 2, 0, (2,), Y),
        (SEND, 2, 0, (0, 1,), IN),
        (SEND, 2, 0, (0,), OUT),
        (SEND, 2, 0, (2,), IN),
        (SEND, 2, 0, (0,), Y),
        (SEND, 2, 0, (1,), OUT),
        (SEND, 2, 0, (3,), OUT),
        (SEND, 2, 0, (3,), IN),
        (SEND, 2, 0, (2,), OUT),
        (SEND, 2, 0, (1,), Y),
    ),
    (MID, 0, 2): (
        (TAKE, 4, 0, (0, 1,), (Y,)),
    ),
    (MID, 0, 4): (
        (TAKE, 4, 0, (2,), (Y,)),
    ),
    (MID, 1, 0): (
        (TAKE, 4, 0, (3,), (Y,)),
        (TAKE, 0, 0, (0, 1, 2, 3,), (Y, OVER,)),
        (TAKE, 5, 0, (0, 1, 2, 3,), (OUT,)),
    ),
    (MID, 1, 2): (
        (TAKE, 1, 0, (0, 1,), (IN,)),
    ),
    (MID, 1, 4): (
        (GIVE, 5, 0, (0, 1, 2, 3,), Y),
        (TAKE, 1, 0, (2, 3,), (IN,)),
    ),
    (MID, 2, 2): (
        (SEND, 2, 0, (3,), Y),
        (JOIN, 4, 3, (0,), IN),
    ),
    (MID, 2, 4): (
        (GIVE, 1, 0, (0, 1, 2, 3,), Y),
        (JOIN, 4, 3, (1, 2,), IN),
    ),
    (MID, 3, 0): (
        (JOIN, 4, 3, (3,), IN),
        (TAKE, 3, 0, (0, 1, 2, 3,), ()),
        (TAKE, 7, 0, (0, 1, 2, 3,), ()),
    ),
    (MID, 3, 2): (
        (JOIN, 0, 3, (0, 1, 2,), OUT),
    ),
    (MID, 3, 4): (
        (GIVE, 3, 0, (0, 1, 2, 3,), Y),
        (JOIN, 0, 3, (3,), OUT),
    ),
    (MID, REST, 0): (
        (JOIN, 2, 7, (0, 1,), None),
        (JOIN, 7, 0, (0,), CROSS),
        (JOIN, 2, 7, (2,), None),
        (JOIN, 7, 0, (1,), CROSS),
        (JOIN, 2, 7, (3,), None),
        (JOIN, 7, 0, (2,), CROSS),
        (JOIN, 2, 3, (0,), None),
        (JOIN, 2, 4, (0,), None),
        (JOIN, 7, 0, (3,), CROSS),
        (JOIN, 2, 3, (1,), None),
        (JOIN, 2, 4, (1,), None),
        (JOIN, 2, 0, (0,), None),
        (JOIN, 2, 3, (2,), None),
        (JOIN, 2, 4, (2,), None),
        (JOIN, 2, 0, (1,), None),
        (JOIN, 2, 3, (3,), None),
        (JOIN, 2, 4, (3,), None),
        (JOIN, 2, 0, (2, 3,), None),
    ),
}


def landing(count, kind, link, slot):
    label, column = divmod(slot, 2)
    if kind + link[0] >= count // 2:
        label = count - 1 - label
    return 2 * label + (column + link[1]) % 2


def links_used(count):
    sent = {
        kind: {
            way
            for (k, _, _), actions in PLAN.items()
            for action, _, _, _, ways in actions
            for way in (ways if action == TAKE else (ways,))
            if k == kind and way is not None
        }
        for kind in (END, MID)
    }
    met = {kind: set(links) for kind, links in sent.items()}
    for kind, links in sent.items():
        for link in links:
            label = kind + link[0]
            label = count - 1 - label if label >= count // 2 else label
            source = landing(count, kind, link, 2 * kind) // 2
            met[label].add((source - label, link[1]))
    return {kind: sorted(links) for kind, links in met.items()}


def split(x):
    high = x.astype(jnp.bfloat16)
    low = (x - high.astype(jnp.float32)).astype(jnp.bfloat16)
    return high, low


def prepare_cache(cache_ref, rope_ref, kcat, vt_hi, vt_lo, fetch=None, first=0, last=None):
    cells, width = cache_ref.shape
    step = STEP

    def body(i, _):
        if fetch is not None:
            fetch(i).wait()
        rows = pl.ds(pl.multiple_of(i * step, step), step)
        block = cache_ref[rows, :]
        high, low = split(block)
        kcat[rows, 0:width] = high
        kcat[rows, width : 2 * width] = low
        turned = block.T
        t_high, t_low = split(turned)
        vt_hi[:, rows] = t_high
        vt_lo[:, rows] = t_low
        rope = rope_ref[:, rows].T
        r_high = rope.astype(jnp.bfloat16).astype(jnp.float32)
        r_low = rope - r_high
        wide = jnp.concatenate([r_high, r_high, r_low, jnp.zeros_like(rope)], axis=1)
        kcat[rows, 2 * width : 2 * width + 4 * rope.shape[1]] = wide.astype(jnp.bfloat16)
        return 0

    lax.fori_loop(first, cells // step if last is None else last, body, 0)


def rope_rows(aux, heads):
    packed = aux[0:heads, :] * FACTOR
    high = packed.astype(jnp.bfloat16).astype(jnp.float32)
    low = packed - high
    half = packed.shape[1] // 2
    blank = jnp.zeros((heads, half), jnp.float32)
    rows = []
    for part in (slice(0, half), slice(half, 2 * half)):
        rows.append(jnp.concatenate([high[:, part], low[:, part], high[:, part], blank], axis=1))
    return jnp.concatenate(rows, axis=0).astype(jnp.bfloat16)


def visit(parts, kcat, vt_hi, vt_lo, s_ref, ph_ref, pl_ref, window):
    cells = kcat.shape[0]
    width = vt_hi.shape[0]
    heads = parts[0][1].shape[0] - 8
    query = jnp.concatenate([p[0] for p in parts], axis=0) * FACTOR
    q_hi, q_lo = split(query)
    rope = jnp.concatenate([rope_rows(p[1], heads) for p in parts], axis=0)
    q_cat = jnp.concatenate([q_hi, q_hi, rope], axis=1)
    starts = jnp.concatenate([p[1][heads : heads + 1, :] - p[2] for p in parts], axis=1)
    extents = jnp.concatenate([p[1][heads + 1 : heads + 2, :] * p[3] for p in parts], axis=1)
    ends = starts + extents
    wrapped = ends - window
    count = query.shape[0]
    peak = jnp.full((1, count), FLOOR, jnp.float32)
    for c in range(cells // CHUNK):
        rows = slice(c * CHUNK, (c + 1) * CHUNK)
        scores = lax.dot_general(kcat[rows, :], q_cat, NT, preferred_element_type=jnp.float32)
        scores += lax.dot_general(
            kcat[rows, 0:width], q_lo, NT, preferred_element_type=jnp.float32
        )
        cell = lax.broadcasted_iota(jnp.int32, (CHUNK, count), 0).astype(jnp.float32) + c * CHUNK
        live = ((cell >= starts) & (cell < ends)) | (cell < wrapped)
        scores = jnp.where(live, scores, DEAD)
        s_ref[rows, 0:count] = scores
        peak = jnp.maximum(peak, jnp.max(scores, axis=0, keepdims=True))
    total = jnp.zeros((1, count), jnp.float32)
    summed = None
    for c in range(cells // CHUNK):
        rows = slice(c * CHUNK, (c + 1) * CHUNK)
        weights = jnp.exp2(s_ref[rows, 0:count] - peak)
        total += jnp.sum(weights, axis=0, keepdims=True)
        high, low = split(weights)
        ph_ref[rows, 0:count] = high
        pl_ref[rows, 0:count] = low
    high = ph_ref[:, 0:count]
    summed = jnp.dot(vt_hi[...], high, preferred_element_type=jnp.float32)
    summed += jnp.dot(vt_hi[...], pl_ref[:, 0:count], preferred_element_type=jnp.float32)
    summed += jnp.dot(vt_lo[...], high, preferred_element_type=jnp.float32)
    return summed, peak, total


def window_kernel(
    size,
    q_ref, aux_ref, cache_ref, rope_ref, out_ref,
    kcat, vt_hi, vt_lo, s_ref, ph_ref, pl_ref,
    q_got, aux_got, sums, stats, sums_got, stats_got,
    q_send, q_recv, a_send, a_recv, o_send, o_recv, t_send, t_recv,
):
    me = lax.axis_index("blk")
    cells = cache_ref.shape[0]
    window = (2 * HOPS + 1) * cells
    distances = [sign * k for k in range(1, HOPS + 1) for sign in (1, -1)]

    def device(distance):
        return {"blk": lax.rem(me + distance + size, size)}

    barrier = pltpu.get_barrier_semaphore()
    for d in distances:
        pl.semaphore_signal(barrier, inc=1, device_id=device(d), device_id_type=MESH)
    pl.semaphore_wait(barrier, 2 * HOPS)

    sent = []
    for i, d in enumerate(distances):
        for source, target, send, recv in (
            (q_ref, q_got, q_send, q_recv),
            (aux_ref, aux_got, a_send, a_recv),
        ):
            copy = pltpu.make_async_remote_copy(
                src_ref=source, dst_ref=target.at[i], send_sem=send.at[i], recv_sem=recv.at[i],
                device_id=device(d), device_id_type=MESH,
            )
            copy.start()
            sent.append(copy)

    prepare_cache(cache_ref, rope_ref, kcat, vt_hi, vt_lo)
    run = functools.partial(
        visit, kcat=kcat, vt_hi=vt_hi, vt_lo=vt_lo, s_ref=s_ref, ph_ref=ph_ref, pl_ref=pl_ref,
        window=window,
    )
    rows = q_ref.shape[0]
    own = run([(q_ref[...], aux_ref[...], float(HOPS * cells), 1.0)])
    sums[2 * HOPS, :, :] = own[0]
    stats[2 * HOPS, 0:1, :] = own[1]
    stats[2 * HOPS, 1:2, :] = own[2]

    def pair(k, _):
        parts = []
        for j, sign in ((0, 1), (1, -1)):
            i = 2 * k + j
            for source, target, send, recv in (
                (q_ref, q_got, q_send, q_recv),
                (aux_ref, aux_got, a_send, a_recv),
            ):
                pltpu.make_async_remote_copy(
                    src_ref=source, dst_ref=target.at[i], send_sem=send.at[i], recv_sem=recv.at[i],
                    device_id=device(1), device_id_type=MESH,
                ).wait_recv()
            slot = HOPS + sign * (k + 1)
            parts.append((q_got[i], aux_got[i], (slot * cells).astype(jnp.float32), 1.0))
        summed, peak, total = run(parts)
        for j, sign in ((0, 1), (1, -1)):
            i = 2 * k + j
            lanes = slice(j * rows, (j + 1) * rows)
            sums[i, :, :] = summed[:, lanes]
            stats[i, 0:1, :] = peak[:, lanes]
            stats[i, 1:2, :] = total[:, lanes]
            for source, target, send, recv in (
                (sums, sums_got, o_send, o_recv),
                (stats, stats_got, t_send, t_recv),
            ):
                pltpu.make_async_remote_copy(
                    src_ref=source.at[i], dst_ref=target.at[i],
                    send_sem=send.at[i], recv_sem=recv.at[i],
                    device_id=device(-sign * (k + 1)), device_id_type=MESH,
                ).start()
        return 0

    lax.fori_loop(0, HOPS, pair, 0)

    for i in range(2 * HOPS):
        for source, target, send, recv in (
            (sums, sums_got, o_send, o_recv),
            (stats, stats_got, t_send, t_recv),
        ):
            copy = pltpu.make_async_remote_copy(
                src_ref=source.at[i], dst_ref=target.at[i],
                send_sem=send.at[i], recv_sem=recv.at[i],
                device_id=device(1), device_id_type=MESH,
            )
            copy.wait_recv()
            copy.wait_send()

    for copy in sent:
        copy.wait_send()

    peak = stats[2 * HOPS, 0:1, :]
    for i in range(2 * HOPS):
        peak = jnp.maximum(peak, stats_got[i, 0:1, :])
    factors = [jnp.exp2(stats[2 * HOPS, 0:1, :] - peak)]
    total = stats[2 * HOPS, 1:2, :] * factors[0]
    for i in range(2 * HOPS):
        factors.append(jnp.exp2(stats_got[i, 0:1, :] - peak))
        total += stats_got[i, 1:2, :] * factors[i + 1]
    width = sums.shape[1]
    for c in range(0, width, 128):
        piece = sums[2 * HOPS, c : c + 128, :] * factors[0]
        for i in range(2 * HOPS):
            piece += sums_got[i, c : c + 128, :] * factors[i + 1]
        out_ref[:, c : c + 128] = (piece / total).T


def line_kernel(
    size,
    q_ref, q_rope_ref, home_ref, length_ref, cache_hbm, rope_ref, out_ref,
    kcat, vt_hi, vt_lo, s_ref, ph_ref, pl_ref,
    cache, q_all, aux_all, acc, got, fac,
    fetch_sem, own_sem, q_send, q_recv, r_send, r_recv,
):
    me = lax.axis_index("blk")
    count = size // 2
    z, y = me // 2, lax.rem(me, 2)
    far = z >= count // 2
    end = (z == 0) | (z == count - 1)
    inward = jnp.where(far, -1, 1)
    cells, width = cache.shape
    rows = q_ref.shape[0]
    window = (2 * HOPS + 1) * cells
    tall = rows // PIECES
    met = links_used(count)
    ways = sorted({link for links in met.values() for link in links})
    devices = {
        link: {
            "blk": 2 * jnp.clip(z + link[0] * inward, 0, count - 1) + (1 - y if link[1] else y)
        }
        for link in ways
    }

    def remote(source, target, send, recv, link):
        return pltpu.make_async_remote_copy(
            src_ref=source, dst_ref=target, send_sem=send, recv_sem=recv,
            device_id=devices[link], device_id_type=MESH,
        )

    def q_part(slot, p):
        if p == PIECES:
            return aux_all.at[slot]
        return q_all.at[slot, pl.ds(p * tall, tall)]

    def q_copy(kind, link, slot, p):
        there = landing(count, kind, link, slot)
        return remote(
            q_part(slot, p), q_part(there, p), q_send.at[ways.index(link), slot, p], q_recv.at[there, p], link
        )

    def parts_of(p):
        return (PIECES, 0) if p == 0 else (p,)

    def q_start(kind, link, slot, p):
        for part in parts_of(p):
            q_copy(kind, link, slot, part).start()

    def q_wait(slot, p):
        for part in parts_of(p):
            piece = q_part(slot, part)
            remote(piece, piece, q_send.at[0, slot, part], q_recv.at[slot, part], Y).wait_recv()

    def r_part(ref, k):
        return ref.at[pl.ds(0, 8 + deep)] if k == 0 else ref.at[pl.ds(8 + k * deep, deep)]

    deep = width // PARTS

    sides = list(range(size))

    def r_copy(kind, link, slot, k):
        there = landing(count, kind, link, slot)
        side = sides.index(landing(count, kind, link, 2 * kind))
        return remote(
            r_part(acc.at[slot], k), r_part(got.at[side, there], k),
            r_send.at[slot, k], r_recv.at[side, there, k], link,
        )

    def merge(slot, side, k):
        piece = r_part(got.at[side, slot], k)
        remote(piece, piece, r_send.at[slot, k], r_recv.at[side, slot, k], Y).wait_recv()
        if k == 0:
            first, second = acc[slot, 0:1, :], got[side, slot, 0:1, :]
            peak = jnp.maximum(first, second)
            first, second = jnp.exp2(first - peak), jnp.exp2(second - peak)
            total = acc[slot, 1:2, :] * first + got[side, slot, 1:2, :] * second
            acc[slot, 0:1, :] = peak
            acc[slot, 1:2, :] = total
            fac[side, slot, 0:1, :] = first
            fac[side, slot, 1:2, :] = second
        else:
            first, second = fac[side, slot, 0:1, :], fac[side, slot, 1:2, :]
        lines = slice(8 + k * deep, 8 + (k + 1) * deep)
        acc[slot, lines, :] = acc[slot, lines, :] * first + got[side, slot, lines, :] * second

    sent_q, sent_r = {END: [], MID: []}, {END: [], MID: []}

    def perform(kind, actions, note):
        for action, slot, source, pieces, link in actions:
            for p in pieces:
                if action == TAKE:
                    q_wait(slot, p)
                if action == JOIN:
                    merge(slot, source, p)
                for way in link if action == TAKE else () if link is None else (link,):
                    if action in (SEND, TAKE):
                        q_start(kind, way, slot, p)
                        note[0].extend((way, slot, part) for part in parts_of(p))
                    else:
                        r_copy(kind, way, slot, p).start()
                        note[1].append((way, slot, p))

    kinds = ((END, end), (MID, jnp.logical_not(end)))

    def run(point, stages, visit=None):
        for kind, here in kinds:
            due = [(k, PLAN[kind, k, point]) for k in stages if (kind, k, point) in PLAN]
            if due:

                @pl.when(here)
                def _(kind=kind, due=due):
                    for k, actions in due:
                        note = (sent_q[kind], sent_r[kind])
                        if visit is None:
                            perform(kind, actions, note)
                        else:
                            pl.when(visit == k)(
                                functools.partial(perform, kind, actions, note)
                            )

    mine = jnp.where(end, 0, 2)
    own_copy = pltpu.make_async_copy(q_ref, q_all.at[mine], own_sem.at[0])
    own_copy.start()

    def fetch(i):
        part = pl.ds(pl.multiple_of(i * STEP, STEP), STEP)
        return pltpu.make_async_copy(cache_hbm.at[part], cache.at[part], fetch_sem.at[i])

    for i in range(cells // STEP):
        fetch(i).start()

    barrier = pltpu.get_barrier_semaphore()
    for kind, here in kinds:

        @pl.when(here)
        def _(kind=kind):
            for link in met[kind]:
                pl.semaphore_signal(
                    barrier, inc=1, device_id=devices[link], device_id_type=MESH
                )

    height, heads, _ = q_rope_ref.shape
    packed = jnp.concatenate([q_rope_ref[i] for i in range(height)], axis=1)
    aux_all[mine, 0:heads, :] = packed
    line = lax.broadcasted_iota(jnp.int32, (8, rows), 0)
    lane = lax.broadcasted_iota(jnp.int32, (8, rows), 1)
    meta = jnp.zeros((8, rows), jnp.float32)
    for i in range(height):
        values = jnp.where(
            line == 0, home_ref[i].astype(jnp.float32), length_ref[i].astype(jnp.float32)
        )
        meta = jnp.where((lane >= i * heads) & (line < 2), values, meta)
    aux_all[mine, heads : heads + 8, :] = meta

    prepare = functools.partial(prepare_cache, cache, rope_ref, kcat, vt_hi, vt_lo, fetch)
    prepare(0, BEFORE)
    own_copy.wait()
    pl.semaphore_wait(barrier, jnp.where(end, len(met[END]), len(met[MID])))
    run(0, (START,))
    prepare(BEFORE, cells // STEP)

    def pick(i, c):
        chosen = jnp.int32(0)
        for kind, here in kinds:
            for k, pair in enumerate(ORDER[kind]):
                chosen = jnp.where(here & (i == k), pair[c], chosen)
        return chosen

    def step(i, _):
        def hook(point):
            run(point, range(len(ORDER[END])), i)

        hook(0)
        parts, slots = [], []
        for c in range(2):
            slot = pick(i, c)
            label = slot // 2
            block = 2 * jnp.where(far, count - 1 - label, label)
            block += jnp.where(lax.rem(slot, 2) == 0, y, 1 - y)
            place = lax.rem(me - block + HOPS + size, size)
            parts.append((q_all[slot], aux_all[slot], (place * cells).astype(jnp.float32)))
            slots.append(slot)
        visit_line(parts, kcat, vt_hi, vt_lo, s_ref, ph_ref, pl_ref, window, acc, slots, hook)
        return 0

    lax.fori_loop(0, len(ORDER[END]), step, 0)
    run(0, (REST,))

    def result(own):
        total = acc[own, 1:2, :]
        for c in range(0, width, 128):
            out_ref[:, c : c + 128] = (acc[own, 8 + c : 8 + c + 128, :] / total).T

    for kind, here in kinds:

        @pl.when(here)
        def _(kind=kind):
            result(0 if kind == END else 2)
            for link, slot, part in sent_q[kind]:
                q_copy(kind, link, slot, part).wait_send()
            for link, slot, k in sent_r[kind]:
                r_copy(kind, link, slot, k).wait_send()


def visit_line(parts, kcat, vt_hi, vt_lo, s_ref, ph_ref, pl_ref, window, acc, slots, hook):
    cells = kcat.shape[0]
    width = vt_hi.shape[0]
    heads = parts[0][1].shape[0] - 8
    query = jnp.concatenate([p[0] for p in parts], axis=0) * FACTOR
    q_hi, q_lo = split(query)
    rope = jnp.concatenate([rope_rows(p[1], heads) for p in parts], axis=0)
    q_cat = jnp.concatenate([q_hi, q_hi, rope], axis=1)
    starts = jnp.concatenate([p[1][heads : heads + 1, :] - p[2] for p in parts], axis=1)
    extents = jnp.concatenate([p[1][heads + 1 : heads + 2, :] for p in parts], axis=1)
    wrapped = starts + extents - window
    whole = wrapped <= 0
    flip = jnp.where(whole, 1.0, -1.0)
    middle = 0.5 * jnp.where(whole, starts + extents - 1, wrapped - 1) + 0.5 * starts
    bound = 0.5 * jnp.where(whole, extents, extents - window)
    count = query.shape[0]
    rows = count // 2
    peak = jnp.full((8, count), FLOOR, jnp.float32)
    chunks = cells // LONG
    for c in range(chunks):
        lines = slice(c * LONG, (c + 1) * LONG)
        scores = lax.dot_general(kcat[lines, :], q_cat, NT, preferred_element_type=jnp.float32)
        scores += lax.dot_general(
            kcat[lines, 0:width], q_lo, NT, preferred_element_type=jnp.float32
        )
        cell = lax.broadcasted_iota(jnp.int32, (LONG, count), 0).astype(jnp.float32)
        live = jnp.abs(cell - (middle - c * LONG)) * flip < bound
        scores = jnp.where(live, scores, DEAD)
        s_ref[lines, :] = scores
        peak = jnp.maximum(peak, jnp.max(scores.reshape(LONG // 8, 8, count), axis=0))
    peak = jnp.max(peak, axis=0, keepdims=True)
    hook(1)
    total = jnp.zeros((8, count), jnp.float32)
    for c in range(chunks):
        lines = slice(c * LONG, (c + 1) * LONG)
        weights = jnp.exp2(s_ref[lines, :] - peak)
        total += jnp.sum(weights.reshape(LONG // 8, 8, count), axis=0)
        high, low = split(weights)
        ph_ref[lines, :] = high
        pl_ref[lines, :] = low
    total = jnp.sum(total, axis=0, keepdims=True)
    for j, slot in enumerate(slots):
        lanes = slice(j * rows, (j + 1) * rows)
        acc[slot, 0:1, :] = peak[:, lanes]
        acc[slot, 1:2, :] = total[:, lanes]
    hook(2)
    turn = width // TURNS
    for h in range(TURNS):
        feats = slice(h * turn, (h + 1) * turn)
        summed = jnp.dot(vt_hi[feats, :], ph_ref[...], preferred_element_type=jnp.float32)
        summed += jnp.dot(vt_hi[feats, :], pl_ref[...], preferred_element_type=jnp.float32)
        summed += jnp.dot(vt_lo[feats, :], ph_ref[...], preferred_element_type=jnp.float32)
        for j, slot in enumerate(slots):
            lanes = slice(j * rows, (j + 1) * rows)
            acc[slot, 8 + h * turn : 8 + (h + 1) * turn, :] = summed[:, lanes]
        hook(3 + h)


def pack_aux(q_rope, home_offset, lengths):
    height, heads, rope = q_rope.shape
    packed = jnp.concatenate([q_rope[i] for i in range(height)], axis=1)
    meta = jnp.stack([home_offset, lengths]).astype(jnp.float32)
    meta = jnp.repeat(meta, heads, axis=1)
    return jnp.concatenate([packed, meta, jnp.zeros((6, height * heads), jnp.float32)], axis=0)


def shards(size, q_latent, q_rope, cache_latent, cache_rope, home_offset, lengths):
    height, heads, width = q_latent.shape
    cells, rope = cache_rope.shape
    rows = height * heads
    flat = q_latent.reshape(rows, width)
    rope_turned = cache_rope.T
    dma = pltpu.SemaphoreType.DMA
    vmem, anywhere = (pl.BlockSpec(memory_space=m) for m in (pltpu.VMEM, pl.ANY))
    working = [
        pltpu.VMEM((cells, 2 * width + 4 * rope), jnp.bfloat16),
        pltpu.VMEM((width, cells), jnp.bfloat16),
        pltpu.VMEM((width, cells), jnp.bfloat16),
        pltpu.VMEM((cells, 2 * rows), jnp.float32),
        pltpu.VMEM((cells, 2 * rows), jnp.bfloat16),
        pltpu.VMEM((cells, 2 * rows), jnp.bfloat16),
    ]
    if size == 2 * HOPS + 2:
        kernel = line_kernel
        smem = pl.BlockSpec(memory_space=pltpu.SMEM)
        in_specs = [anywhere, vmem, smem, smem, anywhere, vmem]
        operands = (flat, q_rope, home_offset, lengths, cache_latent, rope_turned)
        ways = {link for links in links_used(size // 2).values() for link in links}
        scratch = [
            pltpu.VMEM((cells, width), jnp.float32),
            pltpu.VMEM((size, rows, width), jnp.float32),
            pltpu.VMEM((size, heads + 8, rows), jnp.float32),
            pltpu.VMEM((size, width + 8, rows), jnp.float32),
            pltpu.VMEM((size, size, width + 8, rows), jnp.float32),
            pltpu.VMEM((size, size, 8, rows), jnp.float32),
            dma((cells // STEP,)),
            dma((1,)),
            dma((len(ways), size, PIECES + 1)),
            dma((size, PIECES + 1)),
            dma((size, PARTS)),
            dma((size, size, PARTS)),
        ]
    else:
        kernel = window_kernel
        n = 2 * HOPS
        in_specs = [vmem] * 4
        operands = (flat, pack_aux(q_rope, home_offset, lengths), cache_latent, rope_turned)
        scratch = [
            pltpu.VMEM((n, rows, width), jnp.float32),
            pltpu.VMEM((n, heads + 8, rows), jnp.float32),
            pltpu.VMEM((n + 1, width, rows), jnp.float32),
            pltpu.VMEM((n + 1, 8, rows), jnp.float32),
            pltpu.VMEM((n, width, rows), jnp.float32),
            pltpu.VMEM((n, 8, rows), jnp.float32),
        ] + [dma((n,))] * 8
    out = pl.pallas_call(
        functools.partial(kernel, size),
        out_shape=jax.ShapeDtypeStruct((rows, width), jnp.float32),
        in_specs=in_specs,
        out_specs=vmem,
        scratch_shapes=working + scratch,
        compiler_params=pltpu.CompilerParams(
            collective_id=0, has_side_effects=True, vmem_limit_bytes=60 * 1024 * 1024
        ),
    )(*operands)
    return out.reshape(height, heads, width)


def solution(mesh):
    return jax.shard_map(
        functools.partial(shards, mesh.shape["blk"]),
        mesh=mesh,
        in_specs=(
            P(("groups", "blk"), "head", None),
            P(("groups", "blk"), "head", None),
            P(("groups", "blk"), None),
            P(("groups", "blk"), None),
            P(("groups", "blk")),
            P(("groups", "blk")),
        ),
        out_specs=P(("groups", "blk"), "head", None),
        check_vma=False,
    )
```

```python
import functools
import math

import jax
import jax.numpy as jnp
from jax import lax
from jax.experimental import pallas as pl
from jax.experimental.pallas import tpu as pltpu
from jax.sharding import PartitionSpec as P

ROPE = 64
NOPE = 128
HOPS = 3

MESH = pl.DeviceIdType.MESH
FLOOR = -1e30
DEAD = -2e30
FACTOR = math.log2(math.e) / math.sqrt(NOPE + ROPE)
CHUNK = 256
LONG = 512
STEP = 256

NT = (((1,), (1,)), ((), ()))

Y, IN, OUT, OVER, CROSS, FAR = (0, 1), (1, 0), (-1, 0), (2, 0), (2, 1), (3, 0)
END, MID = 0, 1
START, REST = -1, 9
SEND, TAKE, GIVE, JOIN = range(4)
PIECES = 4
PARTS = 4
TURNS = 2
BEFORE = 2
ORDER = {
    END: ((0, 0), (1, 6), (2, 5), (3, 7)),
    MID: ((2, 2), (0, 4), (5, 1), (3, 7)),
}
PLAN = {
    (END, START, 0): (
        (SEND, 0, 0, (3,), Y),
        (SEND, 0, 0, (0,), Y),
        (SEND, 0, 0, (2,), Y),
        (SEND, 0, 0, (3,), IN),
        (SEND, 0, 0, (0, 1, 2,), IN),
    ),
    (END, 0, 2): (
        (SEND, 0, 0, (1,), Y),
    ),
    (END, 1, 0): (
        (TAKE, 2, 0, (0, 1, 2, 3,), (Y,)),
        (TAKE, 6, 0, (0, 1, 2, 3,), (Y,)),
        (TAKE, 1, 0, (0, 1, 2, 3,), ()),
    ),
    (END, 1, 4): (
        (GIVE, 6, 0, (0, 1, 2, 3,), Y),
        (GIVE, 1, 0, (0, 1, 2, 3,), Y),
    ),
    (END, 2, 0): (
        (TAKE, 5, 0, (0, 1, 2, 3,), ()),
    ),
    (END, 2, 4): (
        (GIVE, 5, 0, (0, 1, 2, 3,), IN),
    ),
    (END, 3, 0): (
        (TAKE, 3, 0, (0, 1, 2, 3,), ()),
        (TAKE, 7, 0, (0, 1, 2, 3,), ()),
    ),
    (END, 3, 4): (
        (GIVE, 3, 0, (0, 1, 2, 3,), Y),
        (JOIN, 7, 1, (0, 1, 2, 3,), IN),
    ),
    (END, REST, 0): (
        (JOIN, 2, 1, (0, 1, 2, 3,), IN),
        (JOIN, 0, 5, (0, 1, 2,), None),
        (JOIN, 0, 2, (0, 1,), None),
        (JOIN, 0, 1, (0, 1,), None),
        (JOIN, 0, 2, (2,), None),
        (JOIN, 0, 5, (3,), None),
        (JOIN, 0, 2, (3,), None),
        (JOIN, 0, 1, (2, 3,), None),
    ),
    (MID, START, 0): (
        (SEND, 2, 0, (0, 1,), IN),
        (SEND, 2, 0, (1,), OUT),
        (SEND, 2, 0, (3,), OUT),
        (SEND, 2, 0, (0,), Y),
        (SEND, 2, 0, (2,), OUT),
        (SEND, 2, 0, (2, 3,), IN),
        (SEND, 2, 0, (2,), Y),
        (SEND, 2, 0, (1,), Y),
        (SEND, 2, 0, (0,), OUT),
    ),
    (MID, 0, 1): (
        (TAKE, 4, 0, (0,), (Y,)),
    ),
    (MID, 0, 2): (
        (TAKE, 4, 0, (1,), (Y,)),
        (TAKE, 0, 0, (0,), (Y, OVER,)),
    ),
    (MID, 0, 3): (
        (TAKE, 4, 0, (2,), (Y,)),
        (TAKE, 0, 0, (1,), (Y, OVER,)),
    ),
    (MID, 0, 4): (
        (TAKE, 4, 0, (3,), (Y,)),
        (TAKE, 0, 0, (2, 3,), (Y, OVER,)),
    ),
    (MID, 1, 0): (
        (TAKE, 5, 0, (0,), (OUT,)),
    ),
    (MID, 1, 1): (
        (TAKE, 5, 0, (1,), (OUT,)),
    ),
    (MID, 1, 2): (
        (TAKE, 1, 0, (0,), (IN,)),
    ),
    (MID, 1, 3): (
        (TAKE, 5, 0, (2,), (OUT,)),
    ),
    (MID, 1, 4): (
        (SEND, 2, 0, (3,), Y),
        (TAKE, 1, 0, (1,), (IN,)),
    ),
    (MID, 2, 0): (
        (TAKE, 5, 0, (3,), (OUT,)),
        (TAKE, 1, 0, (2, 3,), (IN,)),
    ),
    (MID, 2, 4): (
        (GIVE, 1, 0, (0, 1, 2, 3,), Y),
    ),
    (MID, 3, 0): (
        (TAKE, 3, 0, (0, 1, 2, 3,), ()),
        (TAKE, 7, 0, (0, 1, 2, 3,), ()),
    ),
    (MID, 3, 3): (
        (JOIN, 0, 3, (0,), OUT),
        (JOIN, 5, 0, (0,), Y),
        (JOIN, 0, 3, (1,), OUT),
    ),
    (MID, 3, 4): (
        (GIVE, 3, 0, (0, 1, 2, 3,), Y),
        (JOIN, 5, 0, (1,), Y),
        (JOIN, 0, 3, (2,), OUT),
        (JOIN, 5, 0, (2,), Y),
        (JOIN, 0, 3, (3,), OUT),
    ),
    (MID, REST, 0): (
        (JOIN, 5, 0, (3,), Y),
        (JOIN, 4, 3, (0,), IN),
        (JOIN, 7, 0, (0, 1, 2, 3,), CROSS),
        (JOIN, 4, 3, (1,), IN),
        (JOIN, 2, 0, (0,), None),
        (JOIN, 4, 3, (2,), IN),
        (JOIN, 2, 0, (1,), None),
        (JOIN, 4, 3, (3,), IN),
        (JOIN, 2, 0, (2, 3,), None),
        (JOIN, 2, 3, (0, 1,), None),
        (JOIN, 2, 4, (0,), None),
        (JOIN, 2, 3, (2, 3,), None),
        (JOIN, 2, 4, (1, 2, 3,), None),
    ),
}


def landing(count, kind, link, slot):
    label, column = divmod(slot, 2)
    if kind + link[0] >= count // 2:
        label = count - 1 - label
    return 2 * label + (column + link[1]) % 2


def links_used(count):
    sent = {
        kind: {
            way
            for (k, _, _), actions in PLAN.items()
            for action, _, _, _, ways in actions
            for way in (ways if action == TAKE else (ways,))
            if k == kind and way is not None
        }
        for kind in (END, MID)
    }
    met = {kind: set(links) for kind, links in sent.items()}
    for kind, links in sent.items():
        for link in links:
            label = kind + link[0]
            label = count - 1 - label if label >= count // 2 else label
            source = landing(count, kind, link, 2 * kind) // 2
            met[label].add((source - label, link[1]))
    return {kind: sorted(links) for kind, links in met.items()}


def split(x):
    high = x.astype(jnp.bfloat16)
    low = (x - high.astype(jnp.float32)).astype(jnp.bfloat16)
    return high, low


def prepare_cache(cache_ref, rope_ref, kcat, vt_hi, vt_lo, fetch=None, first=0, last=None):
    cells, width = cache_ref.shape
    step = STEP

    def body(i, _):
        if fetch is not None:
            fetch(i).wait()
        rows = pl.ds(pl.multiple_of(i * step, step), step)
        block = cache_ref[rows, :]
        high, low = split(block)
        kcat[rows, 0:width] = high
        kcat[rows, width : 2 * width] = low
        turned = block.T
        t_high, t_low = split(turned)
        vt_hi[:, rows] = t_high
        vt_lo[:, rows] = t_low
        rope = rope_ref[:, rows].T
        r_high = rope.astype(jnp.bfloat16).astype(jnp.float32)
        r_low = rope - r_high
        wide = jnp.concatenate([r_high, r_high, r_low, jnp.zeros_like(rope)], axis=1)
        kcat[rows, 2 * width : 2 * width + 4 * rope.shape[1]] = wide.astype(jnp.bfloat16)
        return 0

    lax.fori_loop(first, cells // step if last is None else last, body, 0)


def rope_rows(aux, heads):
    packed = aux[0:heads, :] * FACTOR
    high = packed.astype(jnp.bfloat16).astype(jnp.float32)
    low = packed - high
    half = packed.shape[1] // 2
    blank = jnp.zeros((heads, half), jnp.float32)
    rows = []
    for part in (slice(0, half), slice(half, 2 * half)):
        rows.append(jnp.concatenate([high[:, part], low[:, part], high[:, part], blank], axis=1))
    return jnp.concatenate(rows, axis=0).astype(jnp.bfloat16)


def visit(parts, kcat, vt_hi, vt_lo, s_ref, ph_ref, pl_ref, window):
    cells = kcat.shape[0]
    width = vt_hi.shape[0]
    heads = parts[0][1].shape[0] - 8
    query = jnp.concatenate([p[0] for p in parts], axis=0) * FACTOR
    q_hi, q_lo = split(query)
    rope = jnp.concatenate([rope_rows(p[1], heads) for p in parts], axis=0)
    q_cat = jnp.concatenate([q_hi, q_hi, rope], axis=1)
    starts = jnp.concatenate([p[1][heads : heads + 1, :] - p[2] for p in parts], axis=1)
    extents = jnp.concatenate([p[1][heads + 1 : heads + 2, :] * p[3] for p in parts], axis=1)
    ends = starts + extents
    wrapped = ends - window
    count = query.shape[0]
    peak = jnp.full((1, count), FLOOR, jnp.float32)
    for c in range(cells // CHUNK):
        rows = slice(c * CHUNK, (c + 1) * CHUNK)
        scores = lax.dot_general(kcat[rows, :], q_cat, NT, preferred_element_type=jnp.float32)
        scores += lax.dot_general(
            kcat[rows, 0:width], q_lo, NT, preferred_element_type=jnp.float32
        )
        cell = lax.broadcasted_iota(jnp.int32, (CHUNK, count), 0).astype(jnp.float32) + c * CHUNK
        live = ((cell >= starts) & (cell < ends)) | (cell < wrapped)
        scores = jnp.where(live, scores, DEAD)
        s_ref[rows, 0:count] = scores
        peak = jnp.maximum(peak, jnp.max(scores, axis=0, keepdims=True))
    total = jnp.zeros((1, count), jnp.float32)
    summed = None
    for c in range(cells // CHUNK):
        rows = slice(c * CHUNK, (c + 1) * CHUNK)
        weights = jnp.exp2(s_ref[rows, 0:count] - peak)
        total += jnp.sum(weights, axis=0, keepdims=True)
        high, low = split(weights)
        ph_ref[rows, 0:count] = high
        pl_ref[rows, 0:count] = low
    high = ph_ref[:, 0:count]
    summed = jnp.dot(vt_hi[...], high, preferred_element_type=jnp.float32)
    summed += jnp.dot(vt_hi[...], pl_ref[:, 0:count], preferred_element_type=jnp.float32)
    summed += jnp.dot(vt_lo[...], high, preferred_element_type=jnp.float32)
    return summed, peak, total


def window_kernel(
    size,
    q_ref, aux_ref, cache_ref, rope_ref, out_ref,
    kcat, vt_hi, vt_lo, s_ref, ph_ref, pl_ref,
    q_got, aux_got, sums, stats, sums_got, stats_got,
    q_send, q_recv, a_send, a_recv, o_send, o_recv, t_send, t_recv,
):
    me = lax.axis_index("blk")
    cells = cache_ref.shape[0]
    window = (2 * HOPS + 1) * cells
    distances = [sign * k for k in range(1, HOPS + 1) for sign in (1, -1)]

    def device(distance):
        return {"blk": lax.rem(me + distance + size, size)}

    barrier = pltpu.get_barrier_semaphore()
    for d in distances:
        pl.semaphore_signal(barrier, inc=1, device_id=device(d), device_id_type=MESH)
    pl.semaphore_wait(barrier, 2 * HOPS)

    sent = []
    for i, d in enumerate(distances):
        for source, target, send, recv in (
            (q_ref, q_got, q_send, q_recv),
            (aux_ref, aux_got, a_send, a_recv),
        ):
            copy = pltpu.make_async_remote_copy(
                src_ref=source, dst_ref=target.at[i], send_sem=send.at[i], recv_sem=recv.at[i],
                device_id=device(d), device_id_type=MESH,
            )
            copy.start()
            sent.append(copy)

    prepare_cache(cache_ref, rope_ref, kcat, vt_hi, vt_lo)
    run = functools.partial(
        visit, kcat=kcat, vt_hi=vt_hi, vt_lo=vt_lo, s_ref=s_ref, ph_ref=ph_ref, pl_ref=pl_ref,
        window=window,
    )
    rows = q_ref.shape[0]
    own = run([(q_ref[...], aux_ref[...], float(HOPS * cells), 1.0)])
    sums[2 * HOPS, :, :] = own[0]
    stats[2 * HOPS, 0:1, :] = own[1]
    stats[2 * HOPS, 1:2, :] = own[2]

    def pair(k, _):
        parts = []
        for j, sign in ((0, 1), (1, -1)):
            i = 2 * k + j
            for source, target, send, recv in (
                (q_ref, q_got, q_send, q_recv),
                (aux_ref, aux_got, a_send, a_recv),
            ):
                pltpu.make_async_remote_copy(
                    src_ref=source, dst_ref=target.at[i], send_sem=send.at[i], recv_sem=recv.at[i],
                    device_id=device(1), device_id_type=MESH,
                ).wait_recv()
            slot = HOPS + sign * (k + 1)
            parts.append((q_got[i], aux_got[i], (slot * cells).astype(jnp.float32), 1.0))
        summed, peak, total = run(parts)
        for j, sign in ((0, 1), (1, -1)):
            i = 2 * k + j
            lanes = slice(j * rows, (j + 1) * rows)
            sums[i, :, :] = summed[:, lanes]
            stats[i, 0:1, :] = peak[:, lanes]
            stats[i, 1:2, :] = total[:, lanes]
            for source, target, send, recv in (
                (sums, sums_got, o_send, o_recv),
                (stats, stats_got, t_send, t_recv),
            ):
                pltpu.make_async_remote_copy(
                    src_ref=source.at[i], dst_ref=target.at[i],
                    send_sem=send.at[i], recv_sem=recv.at[i],
                    device_id=device(-sign * (k + 1)), device_id_type=MESH,
                ).start()
        return 0

    lax.fori_loop(0, HOPS, pair, 0)

    for i in range(2 * HOPS):
        for source, target, send, recv in (
            (sums, sums_got, o_send, o_recv),
            (stats, stats_got, t_send, t_recv),
        ):
            copy = pltpu.make_async_remote_copy(
                src_ref=source.at[i], dst_ref=target.at[i],
                send_sem=send.at[i], recv_sem=recv.at[i],
                device_id=device(1), device_id_type=MESH,
            )
            copy.wait_recv()
            copy.wait_send()

    for copy in sent:
        copy.wait_send()

    peak = stats[2 * HOPS, 0:1, :]
    for i in range(2 * HOPS):
        peak = jnp.maximum(peak, stats_got[i, 0:1, :])
    factors = [jnp.exp2(stats[2 * HOPS, 0:1, :] - peak)]
    total = stats[2 * HOPS, 1:2, :] * factors[0]
    for i in range(2 * HOPS):
        factors.append(jnp.exp2(stats_got[i, 0:1, :] - peak))
        total += stats_got[i, 1:2, :] * factors[i + 1]
    width = sums.shape[1]
    for c in range(0, width, 128):
        piece = sums[2 * HOPS, c : c + 128, :] * factors[0]
        for i in range(2 * HOPS):
            piece += sums_got[i, c : c + 128, :] * factors[i + 1]
        out_ref[:, c : c + 128] = (piece / total).T


def line_kernel(
    size,
    q_ref, q_rope_ref, home_ref, length_ref, cache_hbm, rope_ref, out_ref,
    kcat, vt_hi, vt_lo, s_ref, ph_ref, pl_ref,
    cache, q_all, aux_all, acc, got, fac,
    fetch_sem, own_sem, q_send, q_recv, r_send, r_recv,
):
    me = lax.axis_index("blk")
    count = size // 2
    z, y = me // 2, lax.rem(me, 2)
    far = z >= count // 2
    end = (z == 0) | (z == count - 1)
    inward = jnp.where(far, -1, 1)
    cells, width = cache.shape
    rows = q_ref.shape[0]
    window = (2 * HOPS + 1) * cells
    tall = rows // PIECES
    met = links_used(count)
    ways = sorted({link for links in met.values() for link in links})
    devices = {
        link: {
            "blk": 2 * jnp.clip(z + link[0] * inward, 0, count - 1) + (1 - y if link[1] else y)
        }
        for link in ways
    }

    def remote(source, target, send, recv, link):
        return pltpu.make_async_remote_copy(
            src_ref=source, dst_ref=target, send_sem=send, recv_sem=recv,
            device_id=devices[link], device_id_type=MESH,
        )

    def q_part(slot, p):
        if p == PIECES:
            return aux_all.at[slot]
        return q_all.at[slot, pl.ds(p * tall, tall)]

    def q_copy(kind, link, slot, p):
        there = landing(count, kind, link, slot)
        return remote(
            q_part(slot, p), q_part(there, p), q_send.at[ways.index(link), slot, p], q_recv.at[there, p], link
        )

    def parts_of(p):
        return (PIECES, 0) if p == 0 else (p,)

    def q_start(kind, link, slot, p):
        for part in parts_of(p):
            q_copy(kind, link, slot, part).start()

    def q_wait(slot, p):
        for part in parts_of(p):
            piece = q_part(slot, part)
            remote(piece, piece, q_send.at[0, slot, part], q_recv.at[slot, part], Y).wait_recv()

    def r_part(ref, k):
        return ref.at[pl.ds(0, 8 + deep)] if k == 0 else ref.at[pl.ds(8 + k * deep, deep)]

    deep = width // PARTS

    sides = list(range(size))

    def r_copy(kind, link, slot, k):
        there = landing(count, kind, link, slot)
        side = sides.index(landing(count, kind, link, 2 * kind))
        return remote(
            r_part(acc.at[slot], k), r_part(got.at[side, there], k),
            r_send.at[slot, k], r_recv.at[side, there, k], link,
        )

    def merge(slot, side, k):
        piece = r_part(got.at[side, slot], k)
        remote(piece, piece, r_send.at[slot, k], r_recv.at[side, slot, k], Y).wait_recv()
        if k == 0:
            first, second = acc[slot, 0:1, :], got[side, slot, 0:1, :]
            peak = jnp.maximum(first, second)
            first, second = jnp.exp2(first - peak), jnp.exp2(second - peak)
            total = acc[slot, 1:2, :] * first + got[side, slot, 1:2, :] * second
            acc[slot, 0:1, :] = peak
            acc[slot, 1:2, :] = total
            fac[side, slot, 0:1, :] = first
            fac[side, slot, 1:2, :] = second
        else:
            first, second = fac[side, slot, 0:1, :], fac[side, slot, 1:2, :]
        lines = slice(8 + k * deep, 8 + (k + 1) * deep)
        acc[slot, lines, :] = acc[slot, lines, :] * first + got[side, slot, lines, :] * second

    sent_q, sent_r = {END: [], MID: []}, {END: [], MID: []}

    def perform(kind, actions, note):
        for action, slot, source, pieces, link in actions:
            for p in pieces:
                if action == TAKE:
                    q_wait(slot, p)
                if action == JOIN:
                    merge(slot, source, p)
                for way in link if action == TAKE else () if link is None else (link,):
                    if action in (SEND, TAKE):
                        q_start(kind, way, slot, p)
                        note[0].extend((way, slot, part) for part in parts_of(p))
                    else:
                        r_copy(kind, way, slot, p).start()
                        note[1].append((way, slot, p))

    kinds = ((END, end), (MID, jnp.logical_not(end)))

    def run(point, stages, visit=None):
        for kind, here in kinds:
            due = [(k, PLAN[kind, k, point]) for k in stages if (kind, k, point) in PLAN]
            if due:

                @pl.when(here)
                def _(kind=kind, due=due):
                    for k, actions in due:
                        note = (sent_q[kind], sent_r[kind])
                        if visit is None:
                            perform(kind, actions, note)
                        else:
                            pl.when(visit == k)(
                                functools.partial(perform, kind, actions, note)
                            )

    mine = jnp.where(end, 0, 2)
    own_copy = pltpu.make_async_copy(q_ref, q_all.at[mine], own_sem.at[0])
    own_copy.start()

    def fetch(i):
        part = pl.ds(pl.multiple_of(i * STEP, STEP), STEP)
        return pltpu.make_async_copy(cache_hbm.at[part], cache.at[part], fetch_sem.at[i])

    for i in range(cells // STEP):
        fetch(i).start()

    barrier = pltpu.get_barrier_semaphore()
    for kind, here in kinds:

        @pl.when(here)
        def _(kind=kind):
            for link in met[kind]:
                pl.semaphore_signal(
                    barrier, inc=1, device_id=devices[link], device_id_type=MESH
                )

    height, heads, _ = q_rope_ref.shape
    packed = jnp.concatenate([q_rope_ref[i] for i in range(height)], axis=1)
    aux_all[mine, 0:heads, :] = packed
    line = lax.broadcasted_iota(jnp.int32, (8, rows), 0)
    lane = lax.broadcasted_iota(jnp.int32, (8, rows), 1)
    meta = jnp.zeros((8, rows), jnp.float32)
    for i in range(height):
        values = jnp.where(
            line == 0, home_ref[i].astype(jnp.float32), length_ref[i].astype(jnp.float32)
        )
        meta = jnp.where((lane >= i * heads) & (line < 2), values, meta)
    aux_all[mine, heads : heads + 8, :] = meta

    prepare = functools.partial(prepare_cache, cache, rope_ref, kcat, vt_hi, vt_lo, fetch)
    prepare(0, BEFORE)
    own_copy.wait()
    pl.semaphore_wait(barrier, jnp.where(end, len(met[END]), len(met[MID])))
    run(0, (START,))
    prepare(BEFORE, cells // STEP)

    def pick(i, c):
        chosen = jnp.int32(0)
        for kind, here in kinds:
            for k, pair in enumerate(ORDER[kind]):
                chosen = jnp.where(here & (i == k), pair[c], chosen)
        return chosen

    def step(i, _):
        def hook(point):
            run(point, range(len(ORDER[END])), i)

        hook(0)
        parts, slots = [], []
        for c in range(2):
            slot = pick(i, c)
            label = slot // 2
            block = 2 * jnp.where(far, count - 1 - label, label)
            block += jnp.where(lax.rem(slot, 2) == 0, y, 1 - y)
            place = lax.rem(me - block + HOPS + size, size)
            parts.append((q_all[slot], aux_all[slot], (place * cells).astype(jnp.float32)))
            slots.append(slot)
        visit_line(parts, kcat, vt_hi, vt_lo, s_ref, ph_ref, pl_ref, window, acc, slots, hook)
        return 0

    lax.fori_loop(0, len(ORDER[END]), step, 0)
    run(0, (REST,))

    def result(own):
        total = acc[own, 1:2, :]
        for c in range(0, width, 128):
            out_ref[:, c : c + 128] = (acc[own, 8 + c : 8 + c + 128, :] / total).T

    for kind, here in kinds:

        @pl.when(here)
        def _(kind=kind):
            result(0 if kind == END else 2)
            for link, slot, part in sent_q[kind]:
                q_copy(kind, link, slot, part).wait_send()
            for link, slot, k in sent_r[kind]:
                r_copy(kind, link, slot, k).wait_send()


def visit_line(parts, kcat, vt_hi, vt_lo, s_ref, ph_ref, pl_ref, window, acc, slots, hook):
    cells = kcat.shape[0]
    width = vt_hi.shape[0]
    heads = parts[0][1].shape[0] - 8
    query = jnp.concatenate([p[0] for p in parts], axis=0) * FACTOR
    q_hi, q_lo = split(query)
    rope = jnp.concatenate([rope_rows(p[1], heads) for p in parts], axis=0)
    q_cat = jnp.concatenate([q_hi, q_hi, rope], axis=1)
    starts = jnp.concatenate([p[1][heads : heads + 1, :] - p[2] for p in parts], axis=1)
    extents = jnp.concatenate([p[1][heads + 1 : heads + 2, :] for p in parts], axis=1)
    wrapped = starts + extents - window
    whole = wrapped <= 0
    flip = jnp.where(whole, 1.0, -1.0)
    middle = 0.5 * jnp.where(whole, starts + extents - 1, wrapped - 1) + 0.5 * starts
    bound = 0.5 * jnp.where(whole, extents, extents - window)
    count = query.shape[0]
    rows = count // 2
    peak = jnp.full((8, count), FLOOR, jnp.float32)
    chunks = cells // LONG
    for c in range(chunks):
        lines = slice(c * LONG, (c + 1) * LONG)
        scores = lax.dot_general(kcat[lines, :], q_cat, NT, preferred_element_type=jnp.float32)
        scores += lax.dot_general(
            kcat[lines, 0:width], q_lo, NT, preferred_element_type=jnp.float32
        )
        cell = lax.broadcasted_iota(jnp.int32, (LONG, count), 0).astype(jnp.float32)
        live = jnp.abs(cell - (middle - c * LONG)) * flip < bound
        scores = jnp.where(live, scores, DEAD)
        s_ref[lines, :] = scores
        peak = jnp.maximum(peak, jnp.max(scores.reshape(LONG // 8, 8, count), axis=0))
    peak = jnp.max(peak, axis=0, keepdims=True)
    hook(1)
    total = jnp.zeros((8, count), jnp.float32)
    for c in range(chunks):
        lines = slice(c * LONG, (c + 1) * LONG)
        weights = jnp.exp2(s_ref[lines, :] - peak)
        total += jnp.sum(weights.reshape(LONG // 8, 8, count), axis=0)
        high, low = split(weights)
        ph_ref[lines, :] = high
        pl_ref[lines, :] = low
    total = jnp.sum(total, axis=0, keepdims=True)
    for j, slot in enumerate(slots):
        lanes = slice(j * rows, (j + 1) * rows)
        acc[slot, 0:1, :] = peak[:, lanes]
        acc[slot, 1:2, :] = total[:, lanes]
    hook(2)
    turn = width // TURNS
    for h in range(TURNS):
        feats = slice(h * turn, (h + 1) * turn)
        summed = jnp.dot(vt_hi[feats, :], ph_ref[...], preferred_element_type=jnp.float32)
        summed += jnp.dot(vt_hi[feats, :], pl_ref[...], preferred_element_type=jnp.float32)
        summed += jnp.dot(vt_lo[feats, :], ph_ref[...], preferred_element_type=jnp.float32)
        for j, slot in enumerate(slots):
            lanes = slice(j * rows, (j + 1) * rows)
            acc[slot, 8 + h * turn : 8 + (h + 1) * turn, :] = summed[:, lanes]
        hook(3 + h)


def pack_aux(q_rope, home_offset, lengths):
    height, heads, rope = q_rope.shape
    packed = jnp.concatenate([q_rope[i] for i in range(height)], axis=1)
    meta = jnp.stack([home_offset, lengths]).astype(jnp.float32)
    meta = jnp.repeat(meta, heads, axis=1)
    return jnp.concatenate([packed, meta, jnp.zeros((6, height * heads), jnp.float32)], axis=0)


def shards(size, q_latent, q_rope, cache_latent, cache_rope, home_offset, lengths):
    height, heads, width = q_latent.shape
    cells, rope = cache_rope.shape
    rows = height * heads
    flat = q_latent.reshape(rows, width)
    rope_turned = cache_rope.T
    dma = pltpu.SemaphoreType.DMA
    vmem, anywhere = (pl.BlockSpec(memory_space=m) for m in (pltpu.VMEM, pl.ANY))
    working = [
        pltpu.VMEM((cells, 2 * width + 4 * rope), jnp.bfloat16),
        pltpu.VMEM((width, cells), jnp.bfloat16),
        pltpu.VMEM((width, cells), jnp.bfloat16),
        pltpu.VMEM((cells, 2 * rows), jnp.float32),
        pltpu.VMEM((cells, 2 * rows), jnp.bfloat16),
        pltpu.VMEM((cells, 2 * rows), jnp.bfloat16),
    ]
    if size == 2 * HOPS + 2:
        kernel = line_kernel
        smem = pl.BlockSpec(memory_space=pltpu.SMEM)
        in_specs = [anywhere, vmem, smem, smem, anywhere, vmem]
        operands = (flat, q_rope, home_offset, lengths, cache_latent, rope_turned)
        ways = {link for links in links_used(size // 2).values() for link in links}
        scratch = [
            pltpu.VMEM((cells, width), jnp.float32),
            pltpu.VMEM((size, rows, width), jnp.float32),
            pltpu.VMEM((size, heads + 8, rows), jnp.float32),
            pltpu.VMEM((size, width + 8, rows), jnp.float32),
            pltpu.VMEM((size, size, width + 8, rows), jnp.float32),
            pltpu.VMEM((size, size, 8, rows), jnp.float32),
            dma((cells // STEP,)),
            dma((1,)),
            dma((len(ways), size, PIECES + 1)),
            dma((size, PIECES + 1)),
            dma((size, PARTS)),
            dma((size, size, PARTS)),
        ]
    else:
        kernel = window_kernel
        n = 2 * HOPS
        in_specs = [vmem] * 4
        operands = (flat, pack_aux(q_rope, home_offset, lengths), cache_latent, rope_turned)
        scratch = [
            pltpu.VMEM((n, rows, width), jnp.float32),
            pltpu.VMEM((n, heads + 8, rows), jnp.float32),
            pltpu.VMEM((n + 1, width, rows), jnp.float32),
            pltpu.VMEM((n + 1, 8, rows), jnp.float32),
            pltpu.VMEM((n, width, rows), jnp.float32),
            pltpu.VMEM((n, 8, rows), jnp.float32),
        ] + [dma((n,))] * 8
    out = pl.pallas_call(
        functools.partial(kernel, size),
        out_shape=jax.ShapeDtypeStruct((rows, width), jnp.float32),
        in_specs=in_specs,
        out_specs=vmem,
        scratch_shapes=working + scratch,
        compiler_params=pltpu.CompilerParams(
            collective_id=0, has_side_effects=True, vmem_limit_bytes=60 * 1024 * 1024
        ),
    )(*operands)
    return out.reshape(height, heads, width)


def solution(mesh):
    return jax.shard_map(
        functools.partial(shards, mesh.shape["blk"]),
        mesh=mesh,
        in_specs=(
            P(("groups", "blk"), "head", None),
            P(("groups", "blk"), "head", None),
            P(("groups", "blk"), None),
            P(("groups", "blk"), None),
            P(("groups", "blk")),
            P(("groups", "blk")),
        ),
        out_specs=P(("groups", "blk"), "head", None),
        check_vma=False,
    )
```

```python
import functools
import math

import jax
import jax.numpy as jnp
from jax import lax
from jax.experimental import pallas as pl
from jax.experimental.pallas import tpu as pltpu
from jax.sharding import PartitionSpec as P

ROPE = 64
NOPE = 128
HOPS = 3

MESH = pl.DeviceIdType.MESH
FLOOR = -1e30
DEAD = -2e30
FACTOR = math.log2(math.e) / math.sqrt(NOPE + ROPE)
CHUNK = 256
LONG = 512
STEP = 256

NT = (((1,), (1,)), ((), ()))

Y, IN, OUT, OVER, CROSS, FAR = (0, 1), (1, 0), (-1, 0), (2, 0), (2, 1), (3, 0)
END, MID = 0, 1
START, REST = -1, 9
SEND, TAKE, GIVE, JOIN = range(4)
PIECES = 4
PARTS = 4
TURNS = 2
BEFORE = 3
ORDER = {
    END: ((0, 0), (1, 6), (5, 3), (7, 2)),
    MID: ((2, 2), (5, 4), (0, 1), (3, 7)),
}
PLAN = {
    (END, START, 0): (
        (SEND, 0, 0, (3,), Y),
        (SEND, 0, 0, (1,), Y),
        (SEND, 0, 0, (3,), IN),
        (SEND, 0, 0, (1,), IN),
        (SEND, 0, 0, (0,), Y),
        (SEND, 0, 0, (2,), IN),
        (SEND, 0, 0, (2,), Y),
        (SEND, 0, 0, (0,), IN),
    ),
    (END, 0, 2): (
        (TAKE, 2, 0, (0,), (Y,)),
    ),
    (END, 0, 4): (
        (TAKE, 2, 0, (1,), (Y,)),
    ),
    (END, 1, 0): (
        (TAKE, 2, 0, (2, 3,), (Y,)),
        (TAKE, 6, 0, (0, 1, 2, 3,), (Y,)),
        (TAKE, 1, 0, (0, 1, 2, 3,), ()),
    ),
    (END, 1, 4): (
        (GIVE, 1, 0, (0, 1, 2, 3,), Y),
        (GIVE, 6, 0, (0, 1, 2, 3,), Y),
    ),
    (END, 2, 0): (
        (TAKE, 3, 0, (0, 1, 2, 3,), ()),
        (TAKE, 5, 0, (0, 1, 2, 3,), ()),
    ),
    (END, 2, 4): (
        (GIVE, 3, 0, (0, 1, 2, 3,), Y),
        (GIVE, 5, 0, (0, 1, 2, 3,), CROSS),
    ),
    (END, 3, 0): (
        (TAKE, 7, 0, (0, 1, 2, 3,), ()),
    ),
    (END, 3, 4): (
        (JOIN, 7, 1, (0, 1, 2,), IN),
    ),
    (END, REST, 0): (
        (JOIN, 7, 1, (3,), IN),
        (JOIN, 0, 2, (0,), None),
        (JOIN, 2, 1, (0,), IN),
        (JOIN, 0, 2, (1,), None),
        (JOIN, 0, 1, (0, 1,), None),
        (JOIN, 2, 1, (1,), IN),
        (JOIN, 0, 2, (2,), None),
        (JOIN, 2, 1, (2,), IN),
        (JOIN, 0, 2, (3,), None),
        (JOIN, 0, 1, (2, 3,), None),
        (JOIN, 2, 1, (3,), IN),
        (JOIN, 0, 5, (0, 1, 2, 3,), None),
    ),
    (MID, START, 0): (
        (SEND, 2, 0, (2,), Y),
        (SEND, 2, 0, (0, 1,), IN),
        (SEND, 2, 0, (0,), OUT),
        (SEND, 2, 0, (2,), IN),
        (SEND, 2, 0, (0,), Y),
        (SEND, 2, 0, (1,), OUT),
        (SEND, 2, 0, (3,), OUT),
        (SEND, 2, 0, (3,), IN),
        (SEND, 2, 0, (2,), OUT),
        (SEND, 2, 0, (1,), Y),
    ),
    (MID, 0, 2): (
        (TAKE, 4, 0, (0, 1,), (Y,)),
    ),
    (MID, 0, 4): (
        (TAKE, 4, 0, (2,), (Y,)),
    ),
    (MID, 1, 0): (
        (TAKE, 4, 0, (3,), (Y,)),
        (TAKE, 0, 0, (0, 1, 2, 3,), (Y, OVER,)),
        (TAKE, 5, 0, (0, 1, 2, 3,), (OUT,)),
    ),
    (MID, 1, 2): (
        (TAKE, 1, 0, (0, 1,), (IN,)),
    ),
    (MID, 1, 4): (
        (GIVE, 5, 0, (0, 1, 2, 3,), Y),
        (TAKE, 1, 0, (2, 3,), (IN,)),
    ),
    (MID, 2, 2): (
        (SEND, 2, 0, (3,), Y),
        (JOIN, 4, 3, (0,), IN),
    ),
    (MID, 2, 4): (
        (GIVE, 1, 0, (0, 1, 2, 3,), Y),
        (JOIN, 4, 3, (1, 2,), IN),
    ),
    (MID, 3, 0): (
        (JOIN, 4, 3, (3,), IN),
        (TAKE, 3, 0, (0, 1, 2, 3,), ()),
        (TAKE, 7, 0, (0, 1, 2, 3,), ()),
    ),
    (MID, 3, 2): (
        (JOIN, 0, 3, (0, 1, 2,), OUT),
    ),
    (MID, 3, 4): (
        (GIVE, 3, 0, (0, 1, 2, 3,), Y),
        (JOIN, 0, 3, (3,), OUT),
    ),
    (MID, REST, 0): (
        (JOIN, 2, 7, (0, 1,), None),
        (JOIN, 7, 0, (0,), CROSS),
        (JOIN, 2, 7, (2,), None),
        (JOIN, 7, 0, (1,), CROSS),
        (JOIN, 2, 7, (3,), None),
        (JOIN, 7, 0, (2,), CROSS),
        (JOIN, 2, 3, (0,), None),
        (JOIN, 2, 4, (0,), None),
        (JOIN, 7, 0, (3,), CROSS),
        (JOIN, 2, 3, (1,), None),
        (JOIN, 2, 4, (1,), None),
        (JOIN, 2, 0, (0,), None),
        (JOIN, 2, 3, (2,), None),
        (JOIN, 2, 4, (2,), None),
        (JOIN, 2, 0, (1,), None),
        (JOIN, 2, 3, (3,), None),
        (JOIN, 2, 4, (3,), None),
        (JOIN, 2, 0, (2, 3,), None),
    ),
}


def landing(count, kind, link, slot):
    label, column = divmod(slot, 2)
    if kind + link[0] >= count // 2:
        label = count - 1 - label
    return 2 * label + (column + link[1]) % 2


def links_used(count):
    sent = {
        kind: {
            way
            for (k, _, _), actions in PLAN.items()
            for action, _, _, _, ways in actions
            for way in (ways if action == TAKE else (ways,))
            if k == kind and way is not None
        }
        for kind in (END, MID)
    }
    met = {kind: set(links) for kind, links in sent.items()}
    for kind, links in sent.items():
        for link in links:
            label = kind + link[0]
            label = count - 1 - label if label >= count // 2 else label
            source = landing(count, kind, link, 2 * kind) // 2
            met[label].add((source - label, link[1]))
    return {kind: sorted(links) for kind, links in met.items()}


def split(x):
    high = x.astype(jnp.bfloat16)
    low = (x - high.astype(jnp.float32)).astype(jnp.bfloat16)
    return high, low


def prepare_cache(cache_ref, rope_ref, kcat, vt_hi, vt_lo, fetch=None, first=0, last=None):
    cells, width = cache_ref.shape
    step = STEP

    def body(i, _):
        if fetch is not None:
            fetch(i).wait()
        rows = pl.ds(pl.multiple_of(i * step, step), step)
        block = cache_ref[rows, :]
        high, low = split(block)
        kcat[rows, 0:width] = high
        kcat[rows, width : 2 * width] = low
        turned = block.T
        t_high, t_low = split(turned)
        vt_hi[:, rows] = t_high
        vt_lo[:, rows] = t_low
        rope = rope_ref[:, rows].T
        r_high = rope.astype(jnp.bfloat16).astype(jnp.float32)
        r_low = rope - r_high
        wide = jnp.concatenate([r_high, r_high, r_low, jnp.zeros_like(rope)], axis=1)
        kcat[rows, 2 * width : 2 * width + 4 * rope.shape[1]] = wide.astype(jnp.bfloat16)
        return 0

    lax.fori_loop(first, cells // step if last is None else last, body, 0)


def rope_rows(aux, heads):
    packed = aux[0:heads, :] * FACTOR
    high = packed.astype(jnp.bfloat16).astype(jnp.float32)
    low = packed - high
    half = packed.shape[1] // 2
    blank = jnp.zeros((heads, half), jnp.float32)
    rows = []
    for part in (slice(0, half), slice(half, 2 * half)):
        rows.append(jnp.concatenate([high[:, part], low[:, part], high[:, part], blank], axis=1))
    return jnp.concatenate(rows, axis=0).astype(jnp.bfloat16)


def visit(parts, kcat, vt_hi, vt_lo, s_ref, ph_ref, pl_ref, window):
    cells = kcat.shape[0]
    width = vt_hi.shape[0]
    heads = parts[0][1].shape[0] - 8
    query = jnp.concatenate([p[0] for p in parts], axis=0) * FACTOR
    q_hi, q_lo = split(query)
    rope = jnp.concatenate([rope_rows(p[1], heads) for p in parts], axis=0)
    q_cat = jnp.concatenate([q_hi, q_hi, rope], axis=1)
    starts = jnp.concatenate([p[1][heads : heads + 1, :] - p[2] for p in parts], axis=1)
    extents = jnp.concatenate([p[1][heads + 1 : heads + 2, :] * p[3] for p in parts], axis=1)
    ends = starts + extents
    wrapped = ends - window
    count = query.shape[0]
    peak = jnp.full((1, count), FLOOR, jnp.float32)
    for c in range(cells // CHUNK):
        rows = slice(c * CHUNK, (c + 1) * CHUNK)
        scores = lax.dot_general(kcat[rows, :], q_cat, NT, preferred_element_type=jnp.float32)
        scores += lax.dot_general(
            kcat[rows, 0:width], q_lo, NT, preferred_element_type=jnp.float32
        )
        cell = lax.broadcasted_iota(jnp.int32, (CHUNK, count), 0).astype(jnp.float32) + c * CHUNK
        live = ((cell >= starts) & (cell < ends)) | (cell < wrapped)
        scores = jnp.where(live, scores, DEAD)
        s_ref[rows, 0:count] = scores
        peak = jnp.maximum(peak, jnp.max(scores, axis=0, keepdims=True))
    total = jnp.zeros((1, count), jnp.float32)
    summed = None
    for c in range(cells // CHUNK):
        rows = slice(c * CHUNK, (c + 1) * CHUNK)
        weights = jnp.exp2(s_ref[rows, 0:count] - peak)
        total += jnp.sum(weights, axis=0, keepdims=True)
        high, low = split(weights)
        ph_ref[rows, 0:count] = high
        pl_ref[rows, 0:count] = low
    high = ph_ref[:, 0:count]
    summed = jnp.dot(vt_hi[...], high, preferred_element_type=jnp.float32)
    summed += jnp.dot(vt_hi[...], pl_ref[:, 0:count], preferred_element_type=jnp.float32)
    summed += jnp.dot(vt_lo[...], high, preferred_element_type=jnp.float32)
    return summed, peak, total


def window_kernel(
    size,
    q_ref, aux_ref, cache_ref, rope_ref, out_ref,
    kcat, vt_hi, vt_lo, s_ref, ph_ref, pl_ref,
    q_got, aux_got, sums, stats, sums_got, stats_got,
    q_send, q_recv, a_send, a_recv, o_send, o_recv, t_send, t_recv,
):
    me = lax.axis_index("blk")
    cells = cache_ref.shape[0]
    window = (2 * HOPS + 1) * cells
    distances = [sign * k for k in range(1, HOPS + 1) for sign in (1, -1)]

    def device(distance):
        return {"blk": lax.rem(me + distance + size, size)}

    barrier = pltpu.get_barrier_semaphore()
    for d in distances:
        pl.semaphore_signal(barrier, inc=1, device_id=device(d), device_id_type=MESH)
    pl.semaphore_wait(barrier, 2 * HOPS)

    sent = []
    for i, d in enumerate(distances):
        for source, target, send, recv in (
            (q_ref, q_got, q_send, q_recv),
            (aux_ref, aux_got, a_send, a_recv),
        ):
            copy = pltpu.make_async_remote_copy(
                src_ref=source, dst_ref=target.at[i], send_sem=send.at[i], recv_sem=recv.at[i],
                device_id=device(d), device_id_type=MESH,
            )
            copy.start()
            sent.append(copy)

    prepare_cache(cache_ref, rope_ref, kcat, vt_hi, vt_lo)
    run = functools.partial(
        visit, kcat=kcat, vt_hi=vt_hi, vt_lo=vt_lo, s_ref=s_ref, ph_ref=ph_ref, pl_ref=pl_ref,
        window=window,
    )
    rows = q_ref.shape[0]
    own = run([(q_ref[...], aux_ref[...], float(HOPS * cells), 1.0)])
    sums[2 * HOPS, :, :] = own[0]
    stats[2 * HOPS, 0:1, :] = own[1]
    stats[2 * HOPS, 1:2, :] = own[2]

    def pair(k, _):
        parts = []
        for j, sign in ((0, 1), (1, -1)):
            i = 2 * k + j
            for source, target, send, recv in (
                (q_ref, q_got, q_send, q_recv),
                (aux_ref, aux_got, a_send, a_recv),
            ):
                pltpu.make_async_remote_copy(
                    src_ref=source, dst_ref=target.at[i], send_sem=send.at[i], recv_sem=recv.at[i],
                    device_id=device(1), device_id_type=MESH,
                ).wait_recv()
            slot = HOPS + sign * (k + 1)
            parts.append((q_got[i], aux_got[i], (slot * cells).astype(jnp.float32), 1.0))
        summed, peak, total = run(parts)
        for j, sign in ((0, 1), (1, -1)):
            i = 2 * k + j
            lanes = slice(j * rows, (j + 1) * rows)
            sums[i, :, :] = summed[:, lanes]
            stats[i, 0:1, :] = peak[:, lanes]
            stats[i, 1:2, :] = total[:, lanes]
            for source, target, send, recv in (
                (sums, sums_got, o_send, o_recv),
                (stats, stats_got, t_send, t_recv),
            ):
                pltpu.make_async_remote_copy(
                    src_ref=source.at[i], dst_ref=target.at[i],
                    send_sem=send.at[i], recv_sem=recv.at[i],
                    device_id=device(-sign * (k + 1)), device_id_type=MESH,
                ).start()
        return 0

    lax.fori_loop(0, HOPS, pair, 0)

    for i in range(2 * HOPS):
        for source, target, send, recv in (
            (sums, sums_got, o_send, o_recv),
            (stats, stats_got, t_send, t_recv),
        ):
            copy = pltpu.make_async_remote_copy(
                src_ref=source.at[i], dst_ref=target.at[i],
                send_sem=send.at[i], recv_sem=recv.at[i],
                device_id=device(1), device_id_type=MESH,
            )
            copy.wait_recv()
            copy.wait_send()

    for copy in sent:
        copy.wait_send()

    peak = stats[2 * HOPS, 0:1, :]
    for i in range(2 * HOPS):
        peak = jnp.maximum(peak, stats_got[i, 0:1, :])
    factors = [jnp.exp2(stats[2 * HOPS, 0:1, :] - peak)]
    total = stats[2 * HOPS, 1:2, :] * factors[0]
    for i in range(2 * HOPS):
        factors.append(jnp.exp2(stats_got[i, 0:1, :] - peak))
        total += stats_got[i, 1:2, :] * factors[i + 1]
    width = sums.shape[1]
    for c in range(0, width, 128):
        piece = sums[2 * HOPS, c : c + 128, :] * factors[0]
        for i in range(2 * HOPS):
            piece += sums_got[i, c : c + 128, :] * factors[i + 1]
        out_ref[:, c : c + 128] = (piece / total).T


def line_kernel(
    size,
    q_ref, q_rope_ref, home_ref, length_ref, cache_hbm, rope_ref, out_ref,
    kcat, vt_hi, vt_lo, s_ref, ph_ref, pl_ref,
    cache, q_all, aux_all, acc, got, fac,
    fetch_sem, own_sem, q_send, q_recv, r_send, r_recv,
):
    me = lax.axis_index("blk")
    count = size // 2
    z, y = me // 2, lax.rem(me, 2)
    far = z >= count // 2
    end = (z == 0) | (z == count - 1)
    inward = jnp.where(far, -1, 1)
    cells, width = cache.shape
    rows = q_ref.shape[0]
    window = (2 * HOPS + 1) * cells
    tall = rows // PIECES
    met = links_used(count)
    ways = sorted({link for links in met.values() for link in links})
    devices = {
        link: {
            "blk": 2 * jnp.clip(z + link[0] * inward, 0, count - 1) + (1 - y if link[1] else y)
        }
        for link in ways
    }

    def remote(source, target, send, recv, link):
        return pltpu.make_async_remote_copy(
            src_ref=source, dst_ref=target, send_sem=send, recv_sem=recv,
            device_id=devices[link], device_id_type=MESH,
        )

    def q_part(slot, p):
        if p == PIECES:
            return aux_all.at[slot]
        return q_all.at[slot, pl.ds(p * tall, tall)]

    def q_copy(kind, link, slot, p):
        there = landing(count, kind, link, slot)
        return remote(
            q_part(slot, p), q_part(there, p), q_send.at[ways.index(link), slot, p], q_recv.at[there, p], link
        )

    def parts_of(p):
        return (PIECES, 0) if p == 0 else (p,)

    def q_start(kind, link, slot, p):
        for part in parts_of(p):
            q_copy(kind, link, slot, part).start()

    def q_wait(slot, p):
        for part in parts_of(p):
            piece = q_part(slot, part)
            remote(piece, piece, q_send.at[0, slot, part], q_recv.at[slot, part], Y).wait_recv()

    def r_part(ref, k):
        return ref.at[pl.ds(0, 8 + deep)] if k == 0 else ref.at[pl.ds(8 + k * deep, deep)]

    deep = width // PARTS

    sides = list(range(size))

    def r_copy(kind, link, slot, k):
        there = landing(count, kind, link, slot)
        side = sides.index(landing(count, kind, link, 2 * kind))
        return remote(
            r_part(acc.at[slot], k), r_part(got.at[side, there], k),
            r_send.at[slot, k], r_recv.at[side, there, k], link,
        )

    def merge(slot, side, k):
        piece = r_part(got.at[side, slot], k)
        remote(piece, piece, r_send.at[slot, k], r_recv.at[side, slot, k], Y).wait_recv()
        if k == 0:
            first, second = acc[slot, 0:1, :], got[side, slot, 0:1, :]
            peak = jnp.maximum(first, second)
            first, second = jnp.exp2(first - peak), jnp.exp2(second - peak)
            total = acc[slot, 1:2, :] * first + got[side, slot, 1:2, :] * second
            acc[slot, 0:1, :] = peak
            acc[slot, 1:2, :] = total
            fac[side, slot, 0:1, :] = first
            fac[side, slot, 1:2, :] = second
        else:
            first, second = fac[side, slot, 0:1, :], fac[side, slot, 1:2, :]
        lines = slice(8 + k * deep, 8 + (k + 1) * deep)
        acc[slot, lines, :] = acc[slot, lines, :] * first + got[side, slot, lines, :] * second

    sent_q, sent_r = {END: [], MID: []}, {END: [], MID: []}

    def perform(kind, actions, note):
        for action, slot, source, pieces, link in actions:
            for p in pieces:
                if action == TAKE:
                    q_wait(slot, p)
                if action == JOIN:
                    merge(slot, source, p)
                for way in link if action == TAKE else () if link is None else (link,):
                    if action in (SEND, TAKE):
                        q_start(kind, way, slot, p)
                        note[0].extend((way, slot, part) for part in parts_of(p))
                    else:
                        r_copy(kind, way, slot, p).start()
                        note[1].append((way, slot, p))

    kinds = ((END, end), (MID, jnp.logical_not(end)))

    def run(point, stages, visit=None):
        for kind, here in kinds:
            due = [(k, PLAN[kind, k, point]) for k in stages if (kind, k, point) in PLAN]
            if due:

                @pl.when(here)
                def _(kind=kind, due=due):
                    for k, actions in due:
                        note = (sent_q[kind], sent_r[kind])
                        if visit is None:
                            perform(kind, actions, note)
                        else:
                            pl.when(visit == k)(
                                functools.partial(perform, kind, actions, note)
                            )

    mine = jnp.where(end, 0, 2)
    own_copy = pltpu.make_async_copy(q_ref, q_all.at[mine], own_sem.at[0])
    own_copy.start()

    def fetch(i):
        part = pl.ds(pl.multiple_of(i * STEP, STEP), STEP)
        return pltpu.make_async_copy(cache_hbm.at[part], cache.at[part], fetch_sem.at[i])

    for i in range(cells // STEP):
        fetch(i).start()

    barrier = pltpu.get_barrier_semaphore()
    for kind, here in kinds:

        @pl.when(here)
        def _(kind=kind):
            for link in met[kind]:
                pl.semaphore_signal(
                    barrier, inc=1, device_id=devices[link], device_id_type=MESH
                )

    height, heads, _ = q_rope_ref.shape
    packed = jnp.concatenate([q_rope_ref[i] for i in range(height)], axis=1)
    aux_all[mine, 0:heads, :] = packed
    line = lax.broadcasted_iota(jnp.int32, (8, rows), 0)
    lane = lax.broadcasted_iota(jnp.int32, (8, rows), 1)
    meta = jnp.zeros((8, rows), jnp.float32)
    for i in range(height):
        values = jnp.where(
            line == 0, home_ref[i].astype(jnp.float32), length_ref[i].astype(jnp.float32)
        )
        meta = jnp.where((lane >= i * heads) & (line < 2), values, meta)
    aux_all[mine, heads : heads + 8, :] = meta

    prepare = functools.partial(prepare_cache, cache, rope_ref, kcat, vt_hi, vt_lo, fetch)
    prepare(0, BEFORE)
    own_copy.wait()
    pl.semaphore_wait(barrier, jnp.where(end, len(met[END]), len(met[MID])))
    run(0, (START,))
    prepare(BEFORE, cells // STEP)

    def pick(i, c):
        chosen = jnp.int32(0)
        for kind, here in kinds:
            for k, pair in enumerate(ORDER[kind]):
                chosen = jnp.where(here & (i == k), pair[c], chosen)
        return chosen

    def step(i, _):
        def hook(point):
            run(point, range(len(ORDER[END])), i)

        hook(0)
        parts, slots = [], []
        for c in range(2):
            slot = pick(i, c)
            label = slot // 2
            block = 2 * jnp.where(far, count - 1 - label, label)
            block += jnp.where(lax.rem(slot, 2) == 0, y, 1 - y)
            place = lax.rem(me - block + HOPS + size, size)
            parts.append((q_all[slot], aux_all[slot], (place * cells).astype(jnp.float32)))
            slots.append(slot)
        visit_line(parts, kcat, vt_hi, vt_lo, s_ref, ph_ref, pl_ref, window, acc, slots, hook)
        return 0

    lax.fori_loop(0, len(ORDER[END]), step, 0)
    run(0, (REST,))

    def result(own):
        total = acc[own, 1:2, :]
        for c in range(0, width, 128):
            out_ref[:, c : c + 128] = (acc[own, 8 + c : 8 + c + 128, :] / total).T

    for kind, here in kinds:

        @pl.when(here)
        def _(kind=kind):
            result(0 if kind == END else 2)
            for link, slot, part in sent_q[kind]:
                q_copy(kind, link, slot, part).wait_send()
            for link, slot, k in sent_r[kind]:
                r_copy(kind, link, slot, k).wait_send()


def visit_line(parts, kcat, vt_hi, vt_lo, s_ref, ph_ref, pl_ref, window, acc, slots, hook):
    cells = kcat.shape[0]
    width = vt_hi.shape[0]
    heads = parts[0][1].shape[0] - 8
    query = jnp.concatenate([p[0] for p in parts], axis=0) * FACTOR
    q_hi, q_lo = split(query)
    rope = jnp.concatenate([rope_rows(p[1], heads) for p in parts], axis=0)
    q_cat = jnp.concatenate([q_hi, q_hi, rope], axis=1)
    starts = jnp.concatenate([p[1][heads : heads + 1, :] - p[2] for p in parts], axis=1)
    extents = jnp.concatenate([p[1][heads + 1 : heads + 2, :] for p in parts], axis=1)
    wrapped = starts + extents - window
    whole = wrapped <= 0
    flip = jnp.where(whole, 1.0, -1.0)
    middle = 0.5 * jnp.where(whole, starts + extents - 1, wrapped - 1) + 0.5 * starts
    bound = 0.5 * jnp.where(whole, extents, extents - window)
    count = query.shape[0]
    rows = count // 2
    peak = jnp.full((8, count), FLOOR, jnp.float32)
    chunks = cells // LONG
    for c in range(chunks):
        lines = slice(c * LONG, (c + 1) * LONG)
        scores = lax.dot_general(kcat[lines, :], q_cat, NT, preferred_element_type=jnp.float32)
        scores += lax.dot_general(
            kcat[lines, 0:width], q_lo, NT, preferred_element_type=jnp.float32
        )
        cell = lax.broadcasted_iota(jnp.int32, (LONG, count), 0).astype(jnp.float32)
        live = jnp.abs(cell - (middle - c * LONG)) * flip < bound
        scores = jnp.where(live, scores, DEAD)
        s_ref[lines, :] = scores
        peak = jnp.maximum(peak, jnp.max(scores.reshape(LONG // 8, 8, count), axis=0))
    peak = jnp.max(peak, axis=0, keepdims=True)
    hook(1)
    total = jnp.zeros((8, count), jnp.float32)
    for c in range(chunks):
        lines = slice(c * LONG, (c + 1) * LONG)
        weights = jnp.exp2(s_ref[lines, :] - peak)
        total += jnp.sum(weights.reshape(LONG // 8, 8, count), axis=0)
        high, low = split(weights)
        ph_ref[lines, :] = high
        pl_ref[lines, :] = low
    total = jnp.sum(total, axis=0, keepdims=True)
    for j, slot in enumerate(slots):
        lanes = slice(j * rows, (j + 1) * rows)
        acc[slot, 0:1, :] = peak[:, lanes]
        acc[slot, 1:2, :] = total[:, lanes]
    hook(2)
    turn = width // TURNS
    for h in range(TURNS):
        feats = slice(h * turn, (h + 1) * turn)
        summed = jnp.dot(vt_hi[feats, :], ph_ref[...], preferred_element_type=jnp.float32)
        summed += jnp.dot(vt_hi[feats, :], pl_ref[...], preferred_element_type=jnp.float32)
        summed += jnp.dot(vt_lo[feats, :], ph_ref[...], preferred_element_type=jnp.float32)
        for j, slot in enumerate(slots):
            lanes = slice(j * rows, (j + 1) * rows)
            acc[slot, 8 + h * turn : 8 + (h + 1) * turn, :] = summed[:, lanes]
        hook(3 + h)


def pack_aux(q_rope, home_offset, lengths):
    height, heads, rope = q_rope.shape
    packed = jnp.concatenate([q_rope[i] for i in range(height)], axis=1)
    meta = jnp.stack([home_offset, lengths]).astype(jnp.float32)
    meta = jnp.repeat(meta, heads, axis=1)
    return jnp.concatenate([packed, meta, jnp.zeros((6, height * heads), jnp.float32)], axis=0)


def shards(size, q_latent, q_rope, cache_latent, cache_rope, home_offset, lengths):
    height, heads, width = q_latent.shape
    cells, rope = cache_rope.shape
    rows = height * heads
    flat = q_latent.reshape(rows, width)
    rope_turned = cache_rope.T
    dma = pltpu.SemaphoreType.DMA
    vmem, anywhere = (pl.BlockSpec(memory_space=m) for m in (pltpu.VMEM, pl.ANY))
    working = [
        pltpu.VMEM((cells, 2 * width + 4 * rope), jnp.bfloat16),
        pltpu.VMEM((width, cells), jnp.bfloat16),
        pltpu.VMEM((width, cells), jnp.bfloat16),
        pltpu.VMEM((cells, 2 * rows), jnp.float32),
        pltpu.VMEM((cells, 2 * rows), jnp.bfloat16),
        pltpu.VMEM((cells, 2 * rows), jnp.bfloat16),
    ]
    if size == 2 * HOPS + 2:
        kernel = line_kernel
        smem = pl.BlockSpec(memory_space=pltpu.SMEM)
        in_specs = [anywhere, vmem, smem, smem, anywhere, vmem]
        operands = (flat, q_rope, home_offset, lengths, cache_latent, rope_turned)
        ways = {link for links in links_used(size // 2).values() for link in links}
        scratch = [
            pltpu.VMEM((cells, width), jnp.float32),
            pltpu.VMEM((size, rows, width), jnp.float32),
            pltpu.VMEM((size, heads + 8, rows), jnp.float32),
            pltpu.VMEM((size, width + 8, rows), jnp.float32),
            pltpu.VMEM((size, size, width + 8, rows), jnp.float32),
            pltpu.VMEM((size, size, 8, rows), jnp.float32),
            dma((cells // STEP,)),
            dma((1,)),
            dma((len(ways), size, PIECES + 1)),
            dma((size, PIECES + 1)),
            dma((size, PARTS)),
            dma((size, size, PARTS)),
        ]
    else:
        kernel = window_kernel
        n = 2 * HOPS
        in_specs = [vmem] * 4
        operands = (flat, pack_aux(q_rope, home_offset, lengths), cache_latent, rope_turned)
        scratch = [
            pltpu.VMEM((n, rows, width), jnp.float32),
            pltpu.VMEM((n, heads + 8, rows), jnp.float32),
            pltpu.VMEM((n + 1, width, rows), jnp.float32),
            pltpu.VMEM((n + 1, 8, rows), jnp.float32),
            pltpu.VMEM((n, width, rows), jnp.float32),
            pltpu.VMEM((n, 8, rows), jnp.float32),
        ] + [dma((n,))] * 8
    out = pl.pallas_call(
        functools.partial(kernel, size),
        out_shape=jax.ShapeDtypeStruct((rows, width), jnp.float32),
        in_specs=in_specs,
        out_specs=vmem,
        scratch_shapes=working + scratch,
        compiler_params=pltpu.CompilerParams(
            collective_id=0, has_side_effects=True, vmem_limit_bytes=60 * 1024 * 1024
        ),
    )(*operands)
    return out.reshape(height, heads, width)


def solution(mesh):
    return jax.shard_map(
        functools.partial(shards, mesh.shape["blk"]),
        mesh=mesh,
        in_specs=(
            P(("groups", "blk"), "head", None),
            P(("groups", "blk"), "head", None),
            P(("groups", "blk"), None),
            P(("groups", "blk"), None),
            P(("groups", "blk")),
            P(("groups", "blk")),
        ),
        out_specs=P(("groups", "blk"), "head", None),
        check_vma=False,
    )
```
